256 devices in a mesh: pipe: 2 (over z_lo), tensor: 8 (over x, core), dp: 16 (over z_hi, y).
Axes of the slice: x: 4, y: 4, z: 8 (z_hi: 4, z_lo: 2; z = z_hi * 2 + z_lo), core: 2. Of those that a mesh axis runs over, the one named last changes fastest.
Arguments:
- attn_out: bfloat16 [2, 4, 2048, 4096], P('pipe', None, 'dp', 'tensor'), may hold values from -6 to 6
- grad_top: bfloat16 [4, 2048, 4096], P(None, 'dp', 'tensor'), may hold values from -6 to 6
- branch_grad: bfloat16 [2, 4, 2048, 4096], P('pipe', None, 'dp', 'tensor'), may hold values from -6 to 6
- error_prev: bfloat16 [2, 16, 4096, 4096], P('pipe', 'dp', 'tensor'), may hold values from -0.3984375 to 0.3984375
- q_prev: float32 [2, 4096, 64], P('pipe', 'tensor'), may hold values from -6 to 6
Outputs:
- grad_input: bfloat16 [2, 4, 2048, 4096], P('pipe', None, 'dp', 'tensor')
- error_next: bfloat16 [2, 16, 4096, 4096], P('pipe', 'dp', 'tensor')
- p_factor: float32 [2, 4096, 64], P('pipe', 'tensor')
- q_factor: float32 [2, 4096, 64], P('pipe', 'tensor')
The draws below stay inside these ranges and needn't reach their ends.
All inputs are finite; a program needn't handle non-finite values.
Results may differ from the reference program's by a relative error of at most 0.012.
Values may be sent and summed in bfloat16 or wider, within the bound.
No kernel may reach another device: no remote copies, remote signals or barrier semaphores. Data moves between devices by JAX's collectives and lax.ppermute only.
A program may use at most 128 MiB of HBM per device.

```python
import jax
import jax.numpy as jnp
from jax import lax

D = 4096
RANK = 64
MB = 4
TOK_MB = 128
TOKS = 2048
HDALL = 4096
N_PIPE = 2
N_DP = 16


def shard_levels(stream_key, extent, shards, smallest, top_value):
    factor_of = 1.0
    for position, parts in shards:
        heights = jax.random.uniform(jax.random.fold_in(jax.random.fold_in(stream_key, 6), position), (parts,), jnp.float32, smallest / len(shards), top_value / len(shards))
        factor_of = factor_of * jnp.repeat(jnp.exp(heights), extent[position] // parts).reshape((-1,) + (1,) * (len(extent) - 1 - position))
    return factor_of


def noise(rng, shape, deviation, bound, pieces=(), held_as=jnp.bfloat16):
    drawn = deviation * jax.random.normal(rng, shape, jnp.float32)
    if pieces:
        drawn = drawn * shard_levels(rng, shape, pieces, -0.22, 0.18)
    return jnp.clip(drawn, -bound, bound).astype(held_as)


def setup_inputs(seed: int = 0) -> dict:
    splits = jax.random.split(jax.random.key(seed), 6)
    return {
        "attn_out": noise(splits[0], (N_PIPE, MB, TOKS, HDALL), 1.0, 6.0, ((0, 2), (2, 16), (3, 8))),
        "grad_top": noise(splits[1], (MB, TOKS, D), 1.0, 6.0, ((1, 16), (2, 8))),
        "branch_grad": noise(splits[2], (N_PIPE, MB, TOKS, D), 1.0, 6.0, ((0, 2), (2, 16), (3, 8))),
        "error_prev": noise(splits[3], (N_PIPE, N_DP, HDALL, D), 0.05, 0.3984375, ((0, 2), (1, 16), (2, 8))),
        "q_prev": noise(splits[4], (N_PIPE, D, RANK), 1.0, 6.0, ((0, 2), (1, 8)), jnp.float32),
    }


def orthonormal(praw):
    gram = jnp.dot(praw.T, praw, precision=lax.Precision.HIGHEST)
    lower = jnp.linalg.cholesky(gram)
    return lax.linalg.triangular_solve(lower, praw, left_side=False, lower=True, transpose_a=True)

def reference(attn_out, grad_top, branch_grad, error_prev, q_prev):
    scale = 1.0 / (MB * TOK_MB)
    high = lax.Precision.HIGHEST
    out_grad = grad_top
    inputs, errors, pfacts, qfacts = ([], [], [], [])
    for section in reversed(range(N_PIPE)):
        grad_in = (out_grad.astype(jnp.float32) + branch_grad[section].astype(jnp.float32)).astype(jnp.bfloat16)
        acts = attn_out[section].reshape(MB, N_DP, TOK_MB, HDALL).transpose(1, 0, 2, 3)
        grads = out_grad.reshape(MB, N_DP, TOK_MB, D).transpose(1, 0, 2, 3)

        def local(triple):
            act_rep, grad_rep, err_rep = triple
            total = jnp.zeros((HDALL, D), jnp.float32)
            for micro in range(MB):
                total = total + jnp.dot(act_rep[micro].T.astype(jnp.float32), grad_rep[micro].astype(jnp.float32), preferred_element_type=jnp.float32)
            return total * scale + err_rep.astype(jnp.float32)
        mats = lax.map(local, (acts, grads, error_prev[section]))
        qold = q_prev[section]
        praw = jnp.sum(lax.map(lambda mat: jnp.dot(mat, qold, precision=high), mats), axis=0) / N_DP
        phat = orthonormal(praw)
        qnew = jnp.sum(lax.map(lambda mat: jnp.dot(mat.T, phat, precision=high), mats), axis=0) / N_DP
        err = lax.map(lambda mat: (mat - jnp.dot(phat, qnew.T, precision=high)).astype(jnp.bfloat16), mats)
        inputs.insert(0, grad_in)
        errors.insert(0, err)
        pfacts.insert(0, phat)
        qfacts.insert(0, qnew)
        out_grad = grad_in
    return (jnp.stack(inputs), jnp.stack(errors), jnp.stack(pfacts), jnp.stack(qfacts))
```

```python
import jax
import jax.numpy as jnp
from jax import lax
from jax.experimental import pallas as pl
from jax.experimental.pallas import tpu as pltpu
from jax.sharding import Mesh, PartitionSpec as P

BF = jnp.bfloat16
F32 = jnp.float32
HIGH = lax.Precision.HIGHEST
MIB = 1024 * 1024
ANY = pl.BlockSpec(memory_space=pl.ANY)
VMEM = pl.BlockSpec(memory_space=pltpu.VMEM)
SMEM = pl.BlockSpec(memory_space=pltpu.SMEM)


def sds(shape, dtype):
    return jax.ShapeDtypeStruct(shape, dtype)


def params(mib):
    return pltpu.CompilerParams(vmem_limit_bytes=mib * MIB)


def split3(v):
    h = v.astype(BF)
    r = v - h.astype(F32)
    m = r.astype(BF)
    l = (r - m.astype(F32)).astype(BF)
    return jnp.concatenate([h, m, l], axis=0)


def fold3(v):
    n = v.shape[0] // 3
    return v[:n] + (v[n : 2 * n] + v[2 * n :])


def dot(a, b, ca, cb):
    return lax.dot_general(a, b, (((ca,), (cb,)), ((), ())), preferred_element_type=F32)


def grad_kernel(last_ref, top_ref, recv_ref, br_ref, q_ref, g_ref, gin_ref, u_ref):
    last = last_ref[0]

    @pl.when(last == 1)
    def _():
        g_ref[...] = top_ref[...]

    @pl.when(last == 0)
    def _():
        g_ref[...] = recv_ref[...]

    g = g_ref[...]
    gin_ref[...] = (g.astype(F32) + br_ref[...].astype(F32)).astype(BF)
    u_ref[...] = fold3(dot(split3(q_ref[...]), g, 1, 1))


def eq_kernel(idx_ref, qa_ref, qb_ref, act_ref, e_hbm, out_ref, at_ref, e_buf, sems):
    w = e_buf.shape[2]
    cps = []
    for j in range(8):
        cp = pltpu.make_async_copy(
            e_hbm.at[:, pl.ds(pl.multiple_of(idx_ref[j] * w, w), w)], e_buf.at[j], sems.at[j]
        )
        cp.start()
        cps.append(cp)
    at_ref[...] = act_ref[...].T
    acc = None
    for j in range(8):
        q3 = split3(qa_ref[j] if j < 4 else qb_ref[j - 4])
        cps[j].wait()
        part = dot(q3, e_buf[j], 1, 1)
        acc = part if acc is None else acc + part
    out_ref[...] = fold3(acc)


def p_kernel(u0, u1, u2, u3, act_ref, eq_ref, out_ref):
    u = (u0[...] + u2[...]) + (u1[...] + u3[...])
    p = fold3(dot(split3(u), act_ref[...], 1, 0)) * (1.0 / 512.0) + eq_ref[...]
    for k in range(4):
        out_ref[k] = p


def sum_kernel(in_ref, out_ref):
    s = (in_ref[0] + in_ref[2]) + (in_ref[1] + in_ref[3])
    for k in range(4):
        out_ref[k] = s


def put_chunks(out_ref, slot, r, gram):
    for y in range(4):
        out_ref[slot, y, 0:64, :] = r[:, y * 128 : (y + 1) * 128]
        out_ref[slot, y, 64:96, :] = gram


def q_blocks(idx_ref, p3, v3, gram, gs, e_hbm, out_ref, e_buf, g_buf, sems, base):
    w = e_buf.shape[2]
    cps = []
    for k in range(4):
        a = pltpu.make_async_copy(
            e_hbm.at[:, pl.ds(pl.multiple_of(idx_ref[base + k] * w, w), w)], e_buf.at[k], sems.at[k]
        )
        b = pltpu.make_async_copy(gs[k], g_buf.at[k], sems.at[4 + k])
        a.start()
        b.start()
        cps.append((a, b))
    p3, v3, gram = p3(), v3(), gram()
    for k in range(4):
        cps[k][0].wait()
        cps[k][1].wait()
        r = dot(p3, e_buf[k], 1, 0) + dot(v3, g_buf[k], 1, 0) * (1.0 / 512.0)
        put_chunks(out_ref, idx_ref[base + k] // 2, fold3(r), gram)


def q_send_kernel(
    idx_ref, pz_ref, act_ref, g0, g1, g2, g3, e_hbm, out_ref, p_ref, p3_ref, v3_ref, gram_ref, e_buf, g_buf, sems
):
    def get_p3():
        p = ((pz_ref[0] + pz_ref[2]) + (pz_ref[1] + pz_ref[3])) * (1.0 / 16.0)
        p_ref[...] = p
        p3_ref[...] = split3(p)
        return p3_ref[...]

    def get_v3():
        v3_ref[...] = split3(fold3(dot(p3_ref[...], act_ref[...], 1, 1)))
        return v3_ref[...]

    def get_gram():
        p3 = p3_ref[...]
        g = dot(p3, p3[0:64], 1, 1) + (dot(p3, p3[64:128], 1, 1) + dot(p3, p3[128:192], 1, 1))
        g = fold3(g)
        gram_ref[...] = jnp.concatenate([g[0:32], g[32:64]], axis=1)
        return gram_ref[...]

    q_blocks(idx_ref, get_p3, get_v3, get_gram, (g0, g1, g2, g3), e_hbm, out_ref, e_buf, g_buf, sems, 4)


def q_keep_kernel(idx_ref, p3_ref, v3_ref, gram_ref, g0, g1, g2, g3, e_hbm, out_ref, e_buf, g_buf, sems):
    q_blocks(
        idx_ref,
        lambda: p3_ref[...],
        lambda: v3_ref[...],
        lambda: gram_ref[...],
        (g0, g1, g2, g3),
        e_hbm,
        out_ref,
        e_buf,
        g_buf,
        sems,
        0,
    )


def chunk_sum_kernel(in_ref, q_ref, gram_ref):
    s = in_ref[0]
    for k in range(1, 16):
        s = s + in_ref[k]
    q_ref[...] = s[0:64]
    gram_ref[...] = s[64:96]


def factor_kernel(gram_ref, p_ref, phat_ref, ph2_ref, linv_ref):
    gp = gram_ref[...] * 0.25
    n = 64
    left = jnp.concatenate([gp, pltpu.roll(gp, 64, 1)], axis=0)
    row = lax.broadcasted_iota(jnp.int32, (n, 2 * n), 0)
    lane = lax.broadcasted_iota(jnp.int32, (n, 2 * n), 1)
    a = jnp.where(lane < n, left, jnp.where(lane == row + n, 1.0, 0.0))
    for k in range(n):
        d = a[k : k + 1, k : k + 1]
        r = lax.rsqrt(d)
        r = r * (1.5 - 0.5 * d * r * r)
        rowk = a[k : k + 1, :] * r
        f = jnp.where(row > k, a[:, k : k + 1] * r, 0.0)
        a = jnp.where(row == k, rowk, a - f * rowk)
    linv = pltpu.roll(a, 64, 1)[:, 0:n]
    linv_ref[...] = linv
    phat = jnp.dot(linv, p_ref[...], precision=HIGH, preferred_element_type=F32)
    phat_ref[...] = phat
    hi = phat.astype(BF)
    ph2_ref[0:64] = hi
    ph2_ref[64:128] = (phat - hi.astype(F32)).astype(BF)


def q_scale_kernel(q0, q1, q2, q3, linv_ref, out_ref):
    s = ((q0[...] + q2[...]) + (q1[...] + q3[...])) * (1.0 / 16.0)
    q = jnp.dot(linv_ref[...], s, precision=HIGH, preferred_element_type=F32).astype(BF)
    for k in range(16):
        out_ref[k] = q


def error_kernel(
    idx_ref, at_ref, ph2_ref, qa_ref, qb_ref, ga0, ga1, ga2, ga3, gb0, gb1, gb2, gb3, e_hbm, err_hbm, qf_ref,
    e_buf, g_buf, o_buf, sems
):
    w = e_buf.shape[2]
    gs = (ga0, ga1, ga2, ga3, gb0, gb1, gb2, gb3)

    def cols(j):
        return pl.ds(pl.multiple_of(idx_ref[j] * w, w), w)

    cps = []
    for j in range(8):
        a = pltpu.make_async_copy(e_hbm.at[:, cols(j)], e_buf.at[j], sems.at[j])
        b = pltpu.make_async_copy(gs[j], g_buf.at[j], sems.at[8 + j])
        a.start()
        b.start()
        cps.append((a, b))
    at = at_ref[...]
    ph = -(ph2_ref[...].T)
    outs = []
    for j in range(8):
        src = qa_ref if j < 4 else qb_ref
        base = (idx_ref[j] // 2) * 4
        q = jnp.concatenate([src[base + y] for y in range(4)], axis=1)
        if j == 0:
            qf_ref[...] = q.astype(F32)
        q2 = jnp.concatenate([q, q], axis=0)
        cps[j][0].wait()
        cps[j][1].wait()
        m = dot(at, g_buf[j], 1, 0) * (1.0 / 512.0) + e_buf[j].astype(F32)
        o_buf[j] = (m + dot(ph, q2, 1, 0)).astype(BF)
        o = pltpu.make_async_copy(o_buf.at[j], err_hbm.at[:, cols(j)], sems.at[16 + j])
        o.start()
        outs.append(o)
    for o in outs:
        o.wait()


def shift(v, axis, k):
    n = lax.axis_size(axis)
    return lax.ppermute(v, axis, [(i, (i + k) % n) for i in range(n)])


def swap(v):
    return lax.ppermute(v, "core", [(0, 1), (1, 0)])


def exchange(v, axes):
    return lax.all_to_all(v, axes, 0, 0, tiled=True)


def on_device(attn_out, grad_top, branch_grad, error_prev, q_prev):
    x = lax.axis_index("x")
    c = lax.axis_index("core")
    last = (lax.axis_index("pipe") == 1).astype(jnp.int32).reshape(1)
    act = attn_out.reshape(512, 512)
    top = grad_top.reshape(512, 512)
    br = branch_grad.reshape(512, 512)
    err = error_prev.reshape(512, 4096)
    qt = q_prev[0].T
    ks = jnp.arange(4, dtype=jnp.int32)
    xs = (x - ks) % 4
    idx = jnp.concatenate([xs * 2 + c, xs * 2 + (1 - c)]).astype(jnp.int32)

    sent = (top.astype(F32) + br.astype(F32)).astype(BF)
    recv = lax.ppermute(sent, "pipe", [(1, 0)])

    qa = jnp.stack([qt] + [shift(qt, "x", k) for k in (1, 2, 3)])
    qb = swap(qa)

    grad, grad_in, u = pl.pallas_call(
        grad_kernel,
        out_shape=(sds((512, 512), BF), sds((512, 512), BF), sds((64, 512), F32)),
        in_specs=[SMEM, VMEM, VMEM, VMEM, VMEM],
        out_specs=(VMEM, VMEM, VMEM),
        compiler_params=params(16),
        name="grad_kernel",
    )(last, top, recv, br, qt)

    u = u + swap(u)
    us = [u] + [shift(u, "x", k) for k in (1, 2, 3)]

    ga = [grad] + [shift(grad, "x", k) for k in (1, 2, 3)]
    gb = [swap(g) for g in ga]

    eq, act_t = pl.pallas_call(
        eq_kernel,
        out_shape=(sds((64, 512), F32), sds((512, 512), BF)),
        in_specs=[SMEM, VMEM, VMEM, VMEM, ANY],
        out_specs=(VMEM, VMEM),
        scratch_shapes=[pltpu.VMEM((8, 512, 512), BF), pltpu.SemaphoreType.DMA((8,))],
        compiler_params=params(24),
        name="eq_kernel",
    )(idx, qa, qb, act, err)

    p4 = pl.pallas_call(
        p_kernel,
        out_shape=sds((4, 64, 512), F32),
        in_specs=[VMEM] * 6,
        out_specs=VMEM,
        compiler_params=params(16),
        name="p_kernel",
    )(*us, act, eq)
    p4 = exchange(p4, "y")
    p4 = pl.pallas_call(
        sum_kernel, out_shape=sds((4, 64, 512), F32), in_specs=[VMEM], out_specs=VMEM, name="sum_kernel"
    )(p4)
    p4 = exchange(p4, "zhi")

    scratch = [pltpu.VMEM((4, 512, 512), BF), pltpu.VMEM((4, 512, 512), BF), pltpu.SemaphoreType.DMA((8,))]
    send, p, p3, v3, gram = pl.pallas_call(
        q_send_kernel,
        out_shape=(
            sds((4, 4, 96, 128), F32),
            sds((64, 512), F32),
            sds((192, 512), BF),
            sds((192, 512), BF),
            sds((32, 128), F32),
        ),
        in_specs=[SMEM, VMEM, VMEM] + [ANY] * 5,
        out_specs=(VMEM,) * 5,
        scratch_shapes=scratch,
        compiler_params=params(24),
        name="q_send_kernel",
    )(idx, p4, act, *gb, err)
    arrived = swap(send)
    keep = pl.pallas_call(
        q_keep_kernel,
        out_shape=sds((4, 4, 96, 128), F32),
        in_specs=[SMEM, VMEM, VMEM, VMEM] + [ANY] * 5,
        out_specs=VMEM,
        scratch_shapes=scratch,
        compiler_params=params(24),
        name="q_keep_kernel",
    )(idx, p3, v3, gram, *ga, err)
    chunks = exchange((keep + arrived).reshape(16, 96, 128), ("x", "y"))

    q_part, gram = pl.pallas_call(
        chunk_sum_kernel,
        out_shape=(sds((64, 128), F32), sds((32, 128), F32)),
        in_specs=[VMEM],
        out_specs=(VMEM, VMEM),
        name="chunk_sum_kernel",
    )(chunks)
    qs = [q_part] + [shift(q_part, "zhi", k) for k in (1, 2, 3)]
    phat, ph2, linv = pl.pallas_call(
        factor_kernel,
        out_shape=(sds((64, 512), F32), sds((128, 512), BF), sds((64, 64), F32)),
        in_specs=[VMEM, VMEM],
        out_specs=(VMEM, VMEM, VMEM),
        name="factor_kernel",
    )(gram, p)
    q16 = pl.pallas_call(
        q_scale_kernel,
        out_shape=sds((16, 64, 128), BF),
        in_specs=[VMEM] * 5,
        out_specs=VMEM,
        name="q_scale_kernel",
    )(*qs, linv)
    qfa = exchange(q16, ("x", "y"))
    qfb = swap(qfa)

    error_next, q_own = pl.pallas_call(
        error_kernel,
        out_shape=(sds((512, 4096), BF), sds((64, 512), F32)),
        in_specs=[SMEM, VMEM, VMEM, VMEM, VMEM] + [ANY] * 9,
        out_specs=(ANY, VMEM),
        scratch_shapes=[
            pltpu.VMEM((8, 512, 512), BF),
            pltpu.VMEM((8, 512, 512), BF),
            pltpu.VMEM((8, 512, 512), BF),
            pltpu.SemaphoreType.DMA((24,)),
        ],
        compiler_params=params(32),
        name="error_kernel",
    )(idx, act_t, ph2, qfa, qfb, *ga, *gb, err)
    return (
        grad_in.reshape(branch_grad.shape),
        error_next.reshape(error_prev.shape),
        phat.T[None],
        q_own.T[None],
    )


def solution(mesh):
    fine = Mesh(mesh.devices.reshape(2, 4, 2, 4, 4), ("pipe", "x", "core", "zhi", "y"))
    tensor = ("x", "core")
    dp = ("zhi", "y")
    return jax.shard_map(
        on_device,
        mesh=fine,
        in_specs=(
            P("pipe", None, dp, tensor),
            P(None, dp, tensor),
            P("pipe", None, dp, tensor),
            P("pipe", dp, tensor, None),
            P("pipe", tensor, None),
        ),
        out_specs=(
            P("pipe", None, dp, tensor),
            P("pipe", dp, tensor, None),
            P("pipe", tensor, None),
            P("pipe", tensor, None),
        ),
        check_vma=False,
    )
```

```python
import jax
import jax.numpy as jnp
from jax import lax
from jax.experimental import pallas as pl
from jax.experimental.pallas import tpu as pltpu
from jax.sharding import Mesh, PartitionSpec as P

BF = jnp.bfloat16
F32 = jnp.float32
HIGH = lax.Precision.HIGHEST
MIB = 1024 * 1024
ANY = pl.BlockSpec(memory_space=pl.ANY)
VMEM = pl.BlockSpec(memory_space=pltpu.VMEM)
SMEM = pl.BlockSpec(memory_space=pltpu.SMEM)


def sds(shape, dtype):
    return jax.ShapeDtypeStruct(shape, dtype)


def params(mib):
    return pltpu.CompilerParams(vmem_limit_bytes=mib * MIB)


def split3(v):
    h = v.astype(BF)
    r = v - h.astype(F32)
    m = r.astype(BF)
    l = (r - m.astype(F32)).astype(BF)
    return jnp.concatenate([h, m, l], axis=0)


def fold3(v):
    n = v.shape[0] // 3
    return v[:n] + (v[n : 2 * n] + v[2 * n :])


def dot(a, b, ca, cb):
    return lax.dot_general(a, b, (((ca,), (cb,)), ((), ())), preferred_element_type=F32)


def first_kernel(top_ref, br_ref, q_ref, qr_ref, s_ref, ua_ref, ub_ref):
    top = top_ref[...]
    s = (top.astype(F32) + br_ref[...].astype(F32)).astype(BF)
    s_ref[...] = s
    ub_ref[...] = fold3(dot(split3(qr_ref[...]), s, 1, 1))
    ua = fold3(dot(split3(q_ref[...]), top, 1, 1))
    ua_ref[...] = jnp.where(lax.axis_index("pipe") == 1, ua, 0.0)


def grad_kernel(top_ref, recv_ref, s_ref, br_ref, g_ref, gin_ref):
    last = lax.axis_index("pipe")

    @pl.when(last == 1)
    def _():
        g_ref[...] = top_ref[...]
        gin_ref[...] = s_ref[...]

    @pl.when(last == 0)
    def _():
        g = recv_ref[...]
        g_ref[...] = g
        gin_ref[...] = (g.astype(F32) + br_ref[...].astype(F32)).astype(BF)


def block_row(j):
    return lax.rem(lax.axis_index("x") + 4 - j % 4, 4)


def cols(j, w=512):
    c = lax.axis_index("core")
    owner = block_row(j) * 2 + (c if j < 4 else 1 - c)
    return pl.ds(pl.multiple_of(owner * w, w), w)


def eq_kernel(qa_ref, qb_ref, act_ref, e_ref, out_ref, at_ref):
    at_ref[...] = act_ref[...].T
    acc = None
    for j in range(8):
        q3 = split3(qa_ref[j] if j < 4 else qb_ref[j - 4])
        part = dot(q3, e_ref[:, cols(j)], 1, 1)
        acc = part if acc is None else acc + part
    out_ref[...] = fold3(acc)


def p_kernel(u0, u1, u2, u3, act_ref, eq_ref, out_ref):
    u = sum_of((u0, u1, u2, u3))
    p = fold3(dot(split3(u), act_ref[...], 1, 0)) * (1.0 / 512.0) + eq_ref[...]
    out_ref[...] = p


def sum_of(refs):
    a, b, c, d = refs
    return (a[...] + c[...]) + (b[...] + d[...])


def sum_kernel(a, b, c, d, out_ref):
    out_ref[...] = sum_of((a, b, c, d))


def put_chunks(out_ref, slot, r, gram):
    for y in range(4):
        out_ref[slot, y, 0:64, :] = r[:, y * 128 : (y + 1) * 128]
        out_ref[slot, y, 64:96, :] = gram


def half_kernel(e_ref, out_ref):
    for k in range(4):
        out_ref[k] = e_ref[:, cols(4 + k)]


def pv_kernel(z0, z1, z2, z3, act_ref, out_ref):
    p = sum_of((z0, z1, z2, z3)) * (1.0 / 16.0)
    out_ref[0] = p
    out_ref[1] = fold3(dot(split3(p), act_ref[...], 1, 1))


def q_own_kernel(pv_ref, e_ref, out_ref):
    p3 = split3(pv_ref[0])
    for k in range(4):
        out_ref[k] = fold3(dot(p3, e_ref[:, cols(k)], 1, 0))


def q_kernel(pv_ref, pvs_ref, r_ref, es_ref, g0, g1, g2a, g2b, g3, out_ref, gs_ref):
    v3 = split3(pv_ref[1] + pvs_ref[1])
    q3 = split3(pvs_ref[0])

    def gram_of(p3):
        return dot(p3, p3[0:64], 1, 1) + (dot(p3, p3[64:128], 1, 1) + dot(p3, p3[128:192], 1, 1))

    g = fold3(gram_of(split3(pv_ref[0])) + gram_of(q3))
    gram = jnp.concatenate([g[0:32], g[32:64]], axis=1)
    for k, gr in enumerate((g0, g1, None, g3)):
        if k == 2:
            vg = dot(v3[:, 0:256], g2a[...], 1, 0) + dot(v3[:, 256:512], g2b[...], 1, 0)
            gs_ref[k, 0:256] = g2a[...]
            gs_ref[k, 256:512] = g2b[...]
        else:
            vg = dot(v3, gr[...], 1, 0)
            gs_ref[k] = gr[...]
        r = fold3(dot(q3, es_ref[k], 1, 0) + vg * (1.0 / 512.0)) + r_ref[k]
        put_chunks(out_ref, block_row(k), r, gram)


def chunk_sum_kernel(in_ref, q_ref, gram_ref):
    s = in_ref[0]
    for k in range(1, 16):
        s = s + in_ref[k]
    q_ref[...] = s[0:64]
    gram_ref[...] = s[64:96]


def factor_kernel(gram_ref, p_ref, phat_ref, ph2_ref, linv_ref):
    gp = gram_ref[...] * 0.25
    n = 64
    left = jnp.concatenate([gp, pltpu.roll(gp, 64, 1)], axis=0)
    row = lax.broadcasted_iota(jnp.int32, (n, 2 * n), 0)
    lane = lax.broadcasted_iota(jnp.int32, (n, 2 * n), 1)
    a = jnp.where(lane < n, left, jnp.where(lane == row + n, 1.0, 0.0))
    for k in range(n):
        d = a[k : k + 1, k : k + 1]
        r = lax.rsqrt(d)
        r = r * (1.5 - 0.5 * d * r * r)
        rowk = a[k : k + 1, :] * r
        f = jnp.where(row > k, a[:, k : k + 1] * r, 0.0)
        a = jnp.where(row == k, rowk, a - f * rowk)
    linv = pltpu.roll(a, 64, 1)[:, 0:n]
    linv_ref[...] = linv
    phat = jnp.dot(linv, p_ref[0], precision=HIGH, preferred_element_type=F32)
    phat_ref[...] = phat
    hi = phat.astype(BF)
    ph2_ref[0:64] = hi
    ph2_ref[64:128] = (phat - hi.astype(F32)).astype(BF)


def q_scale_kernel(q0, q1, q2, q3, linv_ref, out_ref):
    s = sum_of((q0, q1, q2, q3)) * (1.0 / 16.0)
    q = jnp.dot(linv_ref[...], s, precision=HIGH, preferred_element_type=F32).astype(BF)
    for k in range(16):
        out_ref[k] = q


def matrix_kernel(at_ref, ga_ref, gb_ref, e_ref, m_ref):
    at = at_ref[...]
    for j in range(8):
        g = ga_ref[j] if j < 4 else gb_ref[j - 4]
        m_ref[j] = dot(at, g, 1, 0) * (1.0 / 512.0) + e_ref[:, cols(j)].astype(F32)


def error_kernel(ph2_ref, qa_ref, qb_ref, m_ref, err_hbm, qf_ref, o_buf, sems):
    ph = -(ph2_ref[...].T)
    outs = []
    for j in range(8):
        src = qa_ref if j < 4 else qb_ref
        base = block_row(j) * 4
        q = jnp.concatenate([src[base + y] for y in range(4)], axis=1)
        if j == 0:
            qf_ref[...] = q.astype(F32)
        q2 = jnp.concatenate([q, q], axis=0)
        o_buf[j] = (m_ref[j] + dot(ph, q2, 1, 0)).astype(BF)
        o = pltpu.make_async_copy(o_buf.at[j], err_hbm.at[:, cols(j)], sems.at[j])
        o.start()
        outs.append(o)
    for o in outs:
        o.wait()


def shift(v, axis, k):
    n = lax.axis_size(axis)
    return lax.ppermute(v, axis, [(i, (i + k) % n) for i in range(n)])


def swap(v):
    return lax.ppermute(v, "core", [(0, 1), (1, 0)])


def ring(v, axis):
    return [v] + [shift(v, axis, k) for k in (1, 2, 3)]


def exchange(v, axes):
    return lax.all_to_all(v, axes, 0, 0, tiled=True)


def on_device(attn_out, grad_top, branch_grad, error_prev, q_prev):
    act = attn_out.reshape(512, 512)
    top = grad_top.reshape(512, 512)
    br = branch_grad.reshape(512, 512)
    err = error_prev.reshape(512, 4096)
    qt = q_prev[0].T

    qr = lax.ppermute(qt, "pipe", [(0, 1)])
    qa = jnp.stack(ring(qt, "x"))
    qb = swap(qa)

    sent, ua, ub = pl.pallas_call(
        first_kernel,
        out_shape=(sds((512, 512), BF), sds((64, 512), F32), sds((64, 512), F32)),
        in_specs=[VMEM] * 4,
        out_specs=(VMEM,) * 3,
        compiler_params=params(6),
        name="first_kernel",
    )(top, br, qt, qr)
    err, ua = lax.optimization_barrier((err, ua))
    eh = pl.pallas_call(
        half_kernel,
        out_shape=sds((4, 512, 512), BF),
        in_specs=[VMEM],
        out_specs=VMEM,
        compiler_params=params(10),
        name="half_kernel",
    )(err)
    eh_s = swap(eh)
    u = ua + lax.ppermute(ub, "pipe", [(1, 0)])
    sent, u = lax.optimization_barrier((sent, u))
    recv = lax.ppermute(sent, "pipe", [(1, 0)])
    u = u + swap(u)
    us = ring(u, "x")

    grad, grad_in = pl.pallas_call(
        grad_kernel,
        out_shape=(sds((512, 512), BF), sds((512, 512), BF)),
        in_specs=[VMEM] * 4,
        out_specs=(VMEM,) * 2,
        compiler_params=params(6),
        name="grad_kernel",
    )(top, recv, sent, br)
    grad, eh_s, *us = lax.optimization_barrier((grad, eh_s, *us))
    g1 = shift(grad, "x", 1)
    g3 = shift(grad, "x", 3)

    eq, act_t = pl.pallas_call(
        eq_kernel,
        out_shape=(sds((64, 512), F32), sds((512, 512), BF)),
        in_specs=[VMEM] * 4,
        out_specs=(VMEM, VMEM),
        compiler_params=params(12),
        name="eq_kernel",
    )(qa, qb, act, err)

    part = pl.pallas_call(
        p_kernel,
        out_shape=sds((64, 512), F32),
        in_specs=[VMEM] * 6,
        out_specs=VMEM,
        compiler_params=params(6),
        name="p_kernel",
    )(*us, act, eq)
    part = pl.pallas_call(
        sum_kernel,
        out_shape=sds((64, 512), F32),
        in_specs=[VMEM] * 4,
        out_specs=VMEM,
        compiler_params=params(4),
        name="sum_kernel",
    )(*ring(part, "y"))

    part, g1, g3 = lax.optimization_barrier((part, g1, g3))
    g2a = shift(g1[:256], "x", 1)
    g2b = shift(g3[256:], "x", 3)
    pv = pl.pallas_call(
        pv_kernel,
        out_shape=sds((2, 64, 512), F32),
        in_specs=[VMEM] * 5,
        out_specs=VMEM,
        compiler_params=params(4),
        name="pv_kernel",
    )(*ring(part, "zhi"), act)
    pvs = swap(pv)
    q_own_part = pl.pallas_call(
        q_own_kernel,
        out_shape=sds((4, 64, 512), F32),
        in_specs=[VMEM] * 2,
        out_specs=VMEM,
        compiler_params=params(8),
        name="q_own_kernel",
    )(pv, err)
    chunks, gs = pl.pallas_call(
        q_kernel,
        out_shape=(sds((4, 4, 96, 128), F32), sds((4, 512, 512), BF)),
        in_specs=[VMEM] * 9,
        out_specs=(VMEM, VMEM),
        compiler_params=params(12),
        name="q_kernel",
    )(pv, pvs, q_own_part, eh_s, grad, g1, g2a, g2b, g3)
    gb = swap(gs)
    chunks = exchange(chunks.reshape(16, 96, 128), ("x", "y"))

    q_part, gram = pl.pallas_call(
        chunk_sum_kernel,
        out_shape=(sds((64, 128), F32), sds((32, 128), F32)),
        in_specs=[VMEM],
        out_specs=(VMEM, VMEM),
        compiler_params=params(4),
        name="chunk_sum_kernel",
    )(chunks)
    qs = ring(q_part, "zhi")
    phat, ph2, linv = pl.pallas_call(
        factor_kernel,
        out_shape=(sds((64, 512), F32), sds((128, 512), BF), sds((64, 64), F32)),
        in_specs=[VMEM, VMEM],
        out_specs=(VMEM, VMEM, VMEM),
        compiler_params=params(4),
        name="factor_kernel",
    )(gram, pv)
    act_t, gram = lax.optimization_barrier((act_t, gram))
    matrix = pl.pallas_call(
        matrix_kernel,
        out_shape=sds((8, 512, 512), F32),
        in_specs=[VMEM] * 4,
        out_specs=VMEM,
        compiler_params=params(20),
        name="matrix_kernel",
    )(act_t, gs, gb, err)
    matrix, linv = lax.optimization_barrier((matrix, linv))
    q16 = pl.pallas_call(
        q_scale_kernel,
        out_shape=sds((16, 64, 128), BF),
        in_specs=[VMEM] * 5,
        out_specs=VMEM,
        compiler_params=params(4),
        name="q_scale_kernel",
    )(*qs, linv)
    qfa = exchange(q16, ("x", "y"))
    qfb = swap(qfa)

    error_next, q_own = pl.pallas_call(
        error_kernel,
        out_shape=(sds((512, 4096), BF), sds((64, 512), F32)),
        in_specs=[VMEM] * 4,
        out_specs=(ANY, VMEM),
        scratch_shapes=[pltpu.VMEM((8, 512, 512), BF), pltpu.SemaphoreType.DMA((8,))],
        compiler_params=params(18),
        name="error_kernel",
    )(ph2, qfa, qfb, matrix)
    return (
        grad_in.reshape(branch_grad.shape),
        error_next.reshape(error_prev.shape),
        phat.T[None],
        q_own.T[None],
    )


def solution(mesh):
    fine = Mesh(mesh.devices.reshape(2, 4, 2, 4, 4), ("pipe", "x", "core", "zhi", "y"))
    tensor = ("x", "core")
    dp = ("zhi", "y")
    return jax.shard_map(
        on_device,
        mesh=fine,
        in_specs=(
            P("pipe", None, dp, tensor),
            P(None, dp, tensor),
            P("pipe", None, dp, tensor),
            P("pipe", dp, tensor, None),
            P("pipe", tensor, None),
        ),
        out_specs=(
            P("pipe", None, dp, tensor),
            P("pipe", dp, tensor, None),
            P("pipe", tensor, None),
            P("pipe", tensor, None),
        ),
        check_vma=False,
    )
```

```python
import jax
import jax.numpy as jnp
from jax import lax
from jax.experimental import pallas as pl
from jax.experimental.pallas import tpu as pltpu
from jax.sharding import Mesh, PartitionSpec as P

BF = jnp.bfloat16
F32 = jnp.float32
HIGH = lax.Precision.HIGHEST
MIB = 1024 * 1024
ANY = pl.BlockSpec(memory_space=pl.ANY)
HBM = pl.BlockSpec(memory_space=pltpu.HBM)
VMEM = pl.BlockSpec(memory_space=pltpu.VMEM)
SMEM = pl.BlockSpec(memory_space=pltpu.SMEM)


def sds(shape, dtype):
    return jax.ShapeDtypeStruct(shape, dtype)


def params(mib):
    return pltpu.CompilerParams(vmem_limit_bytes=mib * MIB)


def split3(v):
    h = v.astype(BF)
    r = v - h.astype(F32)
    m = r.astype(BF)
    l = (r - m.astype(F32)).astype(BF)
    return jnp.concatenate([h, m, l], axis=0)


def fold3(v):
    n = v.shape[0] // 3
    return v[:n] + (v[n : 2 * n] + v[2 * n :])


def dot(a, b, ca, cb):
    return lax.dot_general(a, b, (((ca,), (cb,)), ((), ())), preferred_element_type=F32)


def first_kernel(top_ref, br_ref, q_ref, qr_ref, s_ref, ua_ref, ub_ref):
    top = top_ref[...]
    s = (top.astype(F32) + br_ref[...].astype(F32)).astype(BF)
    s_ref[...] = s
    ub_ref[...] = fold3(dot(split3(qr_ref[...]), s, 1, 1))
    ua = fold3(dot(split3(q_ref[...]), top, 1, 1))
    ua_ref[...] = jnp.where(lax.axis_index("pipe") == 1, ua, 0.0)


def grad_kernel(top_ref, recv_ref, s_ref, br_ref, g_ref, gin_ref):
    last = lax.axis_index("pipe")

    @pl.when(last == 1)
    def _():
        g_ref[...] = top_ref[...]
        gin_ref[...] = s_ref[...]

    @pl.when(last == 0)
    def _():
        g = recv_ref[...]
        g_ref[...] = g
        gin_ref[...] = (g.astype(F32) + br_ref[...].astype(F32)).astype(BF)


def block_row(j):
    return lax.rem(lax.axis_index("x") + 4 - j % 4, 4)


def cols(j, w=512):
    c = lax.axis_index("core")
    owner = block_row(j) * 2 + (c if j < 4 else 1 - c)
    return pl.ds(pl.multiple_of(owner * w, w), w)


def eq_kernel(q0, q1, q2, q3, act_ref, e_ref, es_ref, own_ref, sib_ref, at_ref):
    at_ref[...] = act_ref[...].T
    own = sib = None
    for k, q in enumerate((q0, q1, q2, q3)):
        q3 = split3(q[...])
        a = dot(q3, e_ref[:, cols(k)], 1, 1)
        b = dot(q3, es_ref[k], 1, 1)
        own = a if own is None else own + a
        sib = b if sib is None else sib + b
    own_ref[...] = fold3(own)
    sib_ref[...] = fold3(sib)


def p_kernel(u0, u1, u2, u3, act_ref, eq_ref, eqs_ref, out_ref):
    u = sum_of((u0, u1, u2, u3))
    p = fold3(dot(split3(u), act_ref[...], 1, 0)) * (1.0 / 512.0) + (eq_ref[...] + eqs_ref[...])
    out_ref[...] = p


def sum_of(refs):
    a, b, c, d = refs
    return (a[...] + c[...]) + (b[...] + d[...])


def sum_kernel(a, b, c, d, out_ref):
    out_ref[...] = sum_of((a, b, c, d))


def put_chunks(out_ref, slot, r, gram):
    for y in range(4):
        out_ref[slot, y, 0:64, :] = r[:, y * 128 : (y + 1) * 128]
        out_ref[slot, y, 64:96, :] = gram


def run_copies(pairs, sems):
    cps = [pltpu.make_async_copy(s, d, sems.at[i]) for i, (s, d) in enumerate(pairs)]
    for cp in cps:
        cp.start()
    for cp in cps:
        cp.wait()


def load_kernel(q, top, br, q_v, top_v, br_v, sems):
    run_copies(((q, q_v), (top, top_v), (br, br_v)), sems)


def load_error_kernel(e, act, eh_v, e_v, act_v, sems):
    pairs = [(e.at[:, cols(4 + k)], eh_v.at[k]) for k in range(4)]
    run_copies(pairs + [(act, act_v), (e, e_v)], sems)


def pv_kernel(z0, z1, z2, z3, act_ref, out_ref):
    p = sum_of((z0, z1, z2, z3)) * (1.0 / 16.0)
    out_ref[0] = p
    out_ref[1] = fold3(dot(split3(p), act_ref[...], 1, 1))


def q_own_kernel(pv_ref, e_ref, out_ref):
    p3 = split3(pv_ref[0])
    for k in range(4):
        out_ref[k] = fold3(dot(p3, e_ref[:, cols(k)], 1, 0))


def q_kernel(pv_ref, pvs_ref, r_ref, es_ref, g0, g1, g2a, g2b, g3, out_ref, gs_ref):
    v3 = split3(pv_ref[1] + pvs_ref[1])
    q3 = split3(pvs_ref[0])

    def gram_of(p3):
        return dot(p3, p3[0:64], 1, 1) + (dot(p3, p3[64:128], 1, 1) + dot(p3, p3[128:192], 1, 1))

    g = fold3(gram_of(split3(pv_ref[0])) + gram_of(q3))
    gram = jnp.concatenate([g[0:32], g[32:64]], axis=1)
    for k, gr in enumerate((g0, g1, None, g3)):
        if k == 2:
            vg = dot(v3[:, 0:256], g2a[...], 1, 0) + dot(v3[:, 256:512], g2b[...], 1, 0)
            gs_ref[k, 0:256] = g2a[...]
            gs_ref[k, 256:512] = g2b[...]
        else:
            vg = dot(v3, gr[...], 1, 0)
            gs_ref[k] = gr[...]
        r = fold3(dot(q3, es_ref[k], 1, 0) + vg * (1.0 / 512.0)) + r_ref[k]
        put_chunks(out_ref, block_row(k), r, gram)


def chunk_sum_kernel(in_ref, q_ref, gram_ref):
    s = in_ref[0]
    for k in range(1, 16):
        s = s + in_ref[k]
    q_ref[...] = s[0:64]
    gram_ref[...] = s[64:96]


def factor_kernel(gram_ref, p_ref, phat_ref, ph2_ref, linv_ref):
    gp = gram_ref[...] * 0.25
    n = 64
    left = jnp.concatenate([gp, pltpu.roll(gp, 64, 1)], axis=0)
    row = lax.broadcasted_iota(jnp.int32, (n, 2 * n), 0)
    lane = lax.broadcasted_iota(jnp.int32, (n, 2 * n), 1)
    a = jnp.where(lane < n, left, jnp.where(lane == row + n, 1.0, 0.0))
    for k in range(0, n, 8):
        rows = [a[k + i : k + i + 1, :] for i in range(8)]
        fs = [jnp.broadcast_to(a[:, k + i : k + i + 1], (n, 2 * n)) for i in range(8)]
        for i in range(8):
            d = fs[i][k + i : k + i + 1, :]
            r = lax.rsqrt(d)
            r = r * (1.5 - 0.5 * d * r * r)
            rows[i] = rows[i] * r
            fs[i] = fs[i] * r
            for j in range(i + 1, 8):
                m = fs[i][k + j : k + j + 1, :]
                rows[j] = rows[j] - m * rows[i]
                fs[j] = fs[j] - m * fs[i]
        upd = fs[0] * rows[0]
        for i in range(1, 8):
            upd = upd + fs[i] * rows[i]
        block = jnp.concatenate(rows, axis=0)
        parts = [a[:k]] if k else []
        parts.append(block)
        if k + 8 < n:
            parts.append(a[k + 8 :] - upd[k + 8 :])
        a = jnp.concatenate(parts, axis=0) if len(parts) > 1 else block
    linv = pltpu.roll(a, 64, 1)[:, 0:n]
    linv_ref[...] = linv
    phat = jnp.dot(linv, p_ref[0], precision=HIGH, preferred_element_type=F32)
    phat_ref[...] = phat
    hi = phat.astype(BF)
    ph2_ref[0:64] = hi
    ph2_ref[64:128] = (phat - hi.astype(F32)).astype(BF)


def q_scale_kernel(q0, q1, q2, q3, linv_ref, out_ref):
    s = sum_of((q0, q1, q2, q3)) * (1.0 / 16.0)
    q = jnp.dot(linv_ref[...], s, precision=HIGH, preferred_element_type=F32).astype(BF)
    for k in range(16):
        out_ref[k] = q


def matrix_kernel(at_ref, ga_ref, gb_ref, e_ref, m_ref):
    at = at_ref[...]
    for j in range(8):
        g = ga_ref[j] if j < 4 else gb_ref[j - 4]
        m_ref[j] = dot(at, g, 1, 0) * (1.0 / 512.0) + e_ref[:, cols(j)].astype(F32)


def error_half(ph2_ref, q_ref, m_ref, err_hbm, o_buf, sems, base):
    ph = -(ph2_ref[...].T)
    outs = []
    for k in range(4):
        row = block_row(base + k) * 4
        q = jnp.concatenate([q_ref[row + y] for y in range(4)], axis=1)
        q2 = jnp.concatenate([q, q], axis=0)
        o_buf[k] = (m_ref[base + k] + dot(ph, q2, 1, 0)).astype(BF)
        o = pltpu.make_async_copy(o_buf.at[k], err_hbm.at[:, cols(base + k)], sems.at[k])
        o.start()
        outs.append(o)
    return outs


def error_own_kernel(ph2_ref, q_ref, m_ref, err_hbm, qf_ref, o_buf, sems):
    outs = error_half(ph2_ref, q_ref, m_ref, err_hbm, o_buf, sems, 0)
    row = lax.axis_index("x") * 4
    qf_ref[...] = jnp.concatenate([q_ref[row + y] for y in range(4)], axis=1).astype(F32)
    for o in outs:
        o.wait()


def error_sib_kernel(ph2_ref, q_ref, m_ref, _, err_hbm, o_buf, sems):
    for o in error_half(ph2_ref, q_ref, m_ref, err_hbm, o_buf, sems, 4):
        o.wait()


def in_hbm(v):
    return pltpu.with_memory_space_constraint(v, pltpu.HBM)


def shift(v, axis, k):
    n = lax.axis_size(axis)
    return lax.ppermute(v, axis, [(i, (i + k) % n) for i in range(n)])


def swap(v):
    return lax.ppermute(v, "core", [(0, 1), (1, 0)])


def ring(v, axis):
    return [v] + [shift(v, axis, k) for k in (1, 2, 3)]


def exchange(v, axes):
    return lax.all_to_all(v, axes, 0, 0, tiled=True)


def on_device(attn_out, grad_top, branch_grad, error_prev, q_prev):
    act = attn_out.reshape(512, 512)
    top = grad_top.reshape(512, 512)
    br = branch_grad.reshape(512, 512)
    err = error_prev.reshape(512, 4096)
    qt = q_prev[0].T

    qr = lax.ppermute(qt, "pipe", [(0, 1)])
    qx = ring(qt, "x")
    qv, top, br = pl.pallas_call(
        load_kernel,
        out_shape=(sds((64, 512), F32), sds((512, 512), BF), sds((512, 512), BF)),
        in_specs=[HBM] * 3,
        out_specs=(VMEM,) * 3,
        scratch_shapes=[pltpu.SemaphoreType.DMA((3,))],
        compiler_params=params(4),
        name="load_kernel",
    )(*(in_hbm(v) for v in (qt, top, br)))

    eh, err, act = pl.pallas_call(
        load_error_kernel,
        out_shape=(sds((4, 512, 512), BF), sds((512, 4096), BF), sds((512, 512), BF)),
        in_specs=[HBM] * 2,
        out_specs=(VMEM,) * 3,
        scratch_shapes=[pltpu.SemaphoreType.DMA((6,))],
        compiler_params=params(12),
        name="load_error_kernel",
    )(in_hbm(err), in_hbm(act))
    sent, ua, ub = pl.pallas_call(
        first_kernel,
        out_shape=(sds((512, 512), BF), sds((64, 512), F32), sds((64, 512), F32)),
        in_specs=[VMEM] * 4,
        out_specs=(VMEM,) * 3,
        compiler_params=params(6),
        name="first_kernel",
    )(top, br, qv, qr)
    ub, *qx = lax.optimization_barrier((ub, *qx))
    ubr = lax.ppermute(ub, "pipe", [(1, 0)])
    sent, _ = lax.optimization_barrier((sent, eh))
    recv = lax.ppermute(sent, "pipe", [(1, 0)])
    u = ua + ubr
    eh, _ = lax.optimization_barrier((eh, u))
    eh_s = swap(eh)
    u = u + swap(u)
    us = ring(u, "x")
    q0, _ = lax.optimization_barrier((qv, u))
    eq, eq_sib, act_t = pl.pallas_call(
        eq_kernel,
        out_shape=(sds((64, 512), F32), sds((64, 512), F32), sds((512, 512), BF)),
        in_specs=[VMEM] * 7,
        out_specs=(VMEM,) * 3,
        compiler_params=params(12),
        name="eq_kernel",
    )(q0, *qx[1:], act, err, eh_s)
    eqs = swap(eq_sib)
    recv, _ = lax.optimization_barrier((recv, eq))

    grad, grad_in = pl.pallas_call(
        grad_kernel,
        out_shape=(sds((512, 512), BF), sds((512, 512), BF)),
        in_specs=[VMEM] * 4,
        out_specs=(VMEM,) * 2,
        compiler_params=params(6),
        name="grad_kernel",
    )(top, recv, sent, br)
    grad, eqs, *us = lax.optimization_barrier((grad, eqs, *us))
    g1 = shift(grad, "x", 1)
    g3 = shift(grad, "x", 3)

    part = pl.pallas_call(
        p_kernel,
        out_shape=sds((64, 512), F32),
        in_specs=[VMEM] * 7,
        out_specs=VMEM,
        compiler_params=params(6),
        name="p_kernel",
    )(*us, act, eq, eqs)
    part = pl.pallas_call(
        sum_kernel,
        out_shape=sds((64, 512), F32),
        in_specs=[VMEM] * 4,
        out_specs=VMEM,
        compiler_params=params(4),
        name="sum_kernel",
    )(*ring(part, "y"))

    part, g1, g3 = lax.optimization_barrier((part, g1, g3))
    g2a = shift(g1[:256], "x", 1)
    g2b = shift(g3[256:], "x", 3)
    pv = pl.pallas_call(
        pv_kernel,
        out_shape=sds((2, 64, 512), F32),
        in_specs=[VMEM] * 5,
        out_specs=VMEM,
        compiler_params=params(4),
        name="pv_kernel",
    )(*ring(part, "zhi"), act)
    pvs = swap(pv)
    q_own_part = pl.pallas_call(
        q_own_kernel,
        out_shape=sds((4, 64, 512), F32),
        in_specs=[VMEM] * 2,
        out_specs=VMEM,
        compiler_params=params(8),
        name="q_own_kernel",
    )(pv, err)
    chunks, gs = pl.pallas_call(
        q_kernel,
        out_shape=(sds((4, 4, 96, 128), F32), sds((4, 512, 512), BF)),
        in_specs=[VMEM] * 9,
        out_specs=(VMEM, VMEM),
        compiler_params=params(12),
        name="q_kernel",
    )(pv, pvs, q_own_part, eh_s, grad, g1, g2a, g2b, g3)
    gb = swap(gs)
    chunks = exchange(chunks.reshape(16, 96, 128), ("x", "y"))

    q_part, gram = pl.pallas_call(
        chunk_sum_kernel,
        out_shape=(sds((64, 128), F32), sds((32, 128), F32)),
        in_specs=[VMEM],
        out_specs=(VMEM, VMEM),
        compiler_params=params(4),
        name="chunk_sum_kernel",
    )(chunks)
    qs = ring(q_part, "zhi")
    phat, ph2, linv = pl.pallas_call(
        factor_kernel,
        out_shape=(sds((64, 512), F32), sds((128, 512), BF), sds((64, 64), F32)),
        in_specs=[VMEM, VMEM],
        out_specs=(VMEM, VMEM, VMEM),
        compiler_params=params(4),
        name="factor_kernel",
    )(gram, pv)
    act_t, gram = lax.optimization_barrier((act_t, gram))
    matrix = pl.pallas_call(
        matrix_kernel,
        out_shape=sds((8, 512, 512), F32),
        in_specs=[VMEM] * 4,
        out_specs=VMEM,
        compiler_params=params(20),
        name="matrix_kernel",
    )(act_t, gs, gb, err)
    matrix, linv = lax.optimization_barrier((matrix, linv))
    q16 = pl.pallas_call(
        q_scale_kernel,
        out_shape=sds((16, 64, 128), BF),
        in_specs=[VMEM] * 5,
        out_specs=VMEM,
        compiler_params=params(4),
        name="q_scale_kernel",
    )(*qs, linv)
    qfa = exchange(q16, ("x", "y"))
    qfb = swap(qfa)

    scratch = [pltpu.VMEM((4, 512, 512), BF), pltpu.SemaphoreType.DMA((4,))]
    error_next, q_own = pl.pallas_call(
        error_own_kernel,
        out_shape=(sds((512, 4096), BF), sds((64, 512), F32)),
        in_specs=[VMEM] * 3,
        out_specs=(HBM, VMEM),
        scratch_shapes=scratch,
        compiler_params=params(14),
        name="error_own_kernel",
    )(ph2, qfa, matrix)
    error_next = pl.pallas_call(
        error_sib_kernel,
        out_shape=sds((512, 4096), BF),
        in_specs=[VMEM] * 3 + [HBM],
        out_specs=HBM,
        scratch_shapes=scratch,
        input_output_aliases={3: 0},
        compiler_params=params(14),
        name="error_sib_kernel",
    )(ph2, qfb, matrix, error_next)
    return (
        grad_in.reshape(branch_grad.shape),
        error_next.reshape(error_prev.shape),
        phat.T[None],
        q_own.T[None],
    )


def solution(mesh):
    fine = Mesh(mesh.devices.reshape(2, 4, 2, 4, 4), ("pipe", "x", "core", "zhi", "y"))
    tensor = ("x", "core")
    dp = ("zhi", "y")
    return jax.shard_map(
        on_device,
        mesh=fine,
        in_specs=(
            P("pipe", None, dp, tensor),
            P(None, dp, tensor),
            P("pipe", None, dp, tensor),
            P("pipe", dp, tensor, None),
            P("pipe", tensor, None),
        ),
        out_specs=(
            P("pipe", None, dp, tensor),
            P("pipe", dp, tensor, None),
            P("pipe", tensor, None),
            P("pipe", tensor, None),
        ),
        check_vma=False,
    )
```

```python
import jax
import jax.numpy as jnp
from jax import lax
from jax.experimental import pallas as pl
from jax.experimental.pallas import tpu as pltpu
from jax.sharding import Mesh, PartitionSpec as P

BF = jnp.bfloat16
F32 = jnp.float32
HIGH = lax.Precision.HIGHEST
MIB = 1024 * 1024
ANY = pl.BlockSpec(memory_space=pl.ANY)
HBM = pl.BlockSpec(memory_space=pltpu.HBM)
VMEM = pl.BlockSpec(memory_space=pltpu.VMEM)
SMEM = pl.BlockSpec(memory_space=pltpu.SMEM)


LIGHT = pl.CostEstimate(flops=0, transcendentals=0, bytes_accessed=0)


def sds(shape, dtype):
    return jax.ShapeDtypeStruct(shape, dtype)


def params(mib):
    return pltpu.CompilerParams(vmem_limit_bytes=mib * MIB)


def split3(v):
    h = v.astype(BF)
    r = v - h.astype(F32)
    m = r.astype(BF)
    l = (r - m.astype(F32)).astype(BF)
    return jnp.concatenate([h, m, l], axis=0)


def fold3(v):
    n = v.shape[0] // 3
    return v[:n] + (v[n : 2 * n] + v[2 * n :])


def dot(a, b, ca, cb):
    return lax.dot_general(a, b, (((ca,), (cb,)), ((), ())), preferred_element_type=F32)


def u_kernel(top_ref, recv_ref, q_ref, g_ref, u_ref):
    last = lax.axis_index("pipe")

    @pl.when(last == 1)
    def _():
        g_ref[...] = top_ref[...]

    @pl.when(last == 0)
    def _():
        g_ref[...] = recv_ref[...]

    u_ref[...] = fold3(dot(split3(q_ref[...]), g_ref[...], 1, 1))


def grad_in_kernel(g_ref, br_ref, gin_ref):
    gin_ref[...] = (g_ref[...].astype(F32) + br_ref[...].astype(F32)).astype(BF)


def block_row(j):
    return lax.rem(lax.axis_index("x") + 4 - j % 4, 4)


def cols(j, w=512):
    c = lax.axis_index("core")
    owner = block_row(j) * 2 + (c if j < 4 else 1 - c)
    return pl.ds(pl.multiple_of(owner * w, w), w)


def eq_kernel(q0, q1, q2, q3, act_ref, e_ref, es_ref, own_ref, sib_ref, at_ref):
    at_ref[...] = act_ref[...].T
    own = sib = None
    for k, q in enumerate((q0, q1, q2, q3)):
        q3 = split3(q[...])
        a = dot(q3, e_ref[k], 1, 1)
        b = dot(q3, es_ref[k], 1, 1)
        own = a if own is None else own + a
        sib = b if sib is None else sib + b
    own_ref[...] = fold3(own)
    sib_ref[...] = fold3(sib)


def p_kernel(u0, u1, u2, u3, act_ref, eq_ref, eqs_ref, out_ref):
    u = sum_of((u0, u1, u2, u3))
    p = fold3(dot(split3(u), act_ref[...], 1, 0)) * (1.0 / 512.0) + (eq_ref[...] + eqs_ref[...])
    out_ref[...] = p


def sum_of(refs):
    a, b, c, d = refs
    return (a[...] + c[...]) + (b[...] + d[...])


def sum_kernel(a, b, c, d, out_ref):
    out_ref[...] = sum_of((a, b, c, d))


def put_chunks(out_ref, slot, r, gram):
    for y in range(4):
        out_ref[slot, y, 0:64, :] = r[:, y * 128 : (y + 1) * 128]
        out_ref[slot, y, 64:72, :] = gram


def run_copies(pairs, sems):
    cps = [pltpu.make_async_copy(s, d, sems.at[i]) for i, (s, d) in enumerate(pairs)]
    for cp in cps:
        cp.start()
    for cp in cps:
        cp.wait()


def load_kernel(q, top, br, q_v, top_v, br_v, s_v, sems):
    run_copies(((q, q_v), (top, top_v), (br, br_v)), sems)
    s_v[...] = (top_v[...].astype(F32) + br_v[...].astype(F32)).astype(BF)


def load_error_kernel(e, act, eh_v, e_v, act_v, sems):
    pairs = [(e.at[:, cols(4 + k)], eh_v.at[k]) for k in range(4)]
    pairs += [(e.at[:, cols(k)], e_v.at[k]) for k in range(4)]
    run_copies(pairs + [(act, act_v)], sems)


def pv_kernel(z0, z1, z2, z3, act_ref, out_ref):
    p = sum_of((z0, z1, z2, z3)) * (1.0 / 16.0)
    out_ref[0] = p
    out_ref[1] = fold3(dot(split3(p), act_ref[...], 1, 1))


def q_own_kernel(pv_ref, e_ref, out_ref):
    p3 = split3(pv_ref[0])
    for k in range(4):
        out_ref[k] = fold3(dot(p3, e_ref[k], 1, 0))


def q_kernel(pv_ref, pvs_ref, r_ref, es_ref, g0, g1, g2a, g2b, g3, out_ref, gs_ref, gram_scr):
    v3 = split3(pv_ref[1] + pvs_ref[1])
    q3 = split3(pvs_ref[0])

    def gram_of(p3):
        return dot(p3, p3[0:64], 1, 1) + (dot(p3, p3[64:128], 1, 1) + dot(p3, p3[128:192], 1, 1))

    g = fold3(gram_of(split3(pv_ref[0])) + gram_of(q3))
    gram_scr[...] = jnp.concatenate([g[0:32], g[32:64]], axis=1)
    gram = gram_scr[pl.ds(pl.multiple_of(lax.axis_index("y") * 8, 8), 8), :]
    for k, gr in enumerate((g0, g1, None, g3)):
        if k == 2:
            vg = dot(v3[:, 0:256], g2a[...], 1, 0) + dot(v3[:, 256:512], g2b[...], 1, 0)
            gs_ref[k, 0:256] = g2a[...]
            gs_ref[k, 256:512] = g2b[...]
        else:
            vg = dot(v3, gr[...], 1, 0)
            gs_ref[k] = gr[...]
        r = fold3(dot(q3, es_ref[k], 1, 0) + vg * (1.0 / 512.0)) + r_ref[k]
        put_chunks(out_ref, block_row(k), r, gram)


def chunk_sum_kernel(in_ref, q_ref, gram_ref):
    s = in_ref[0, 0:64]
    for k in range(1, 16):
        s = s + in_ref[k, 0:64]
    q_ref[...] = s
    for y in range(4):
        g = (in_ref[y, 64:72] + in_ref[4 + y, 64:72]) + (in_ref[8 + y, 64:72] + in_ref[12 + y, 64:72])
        gram_ref[8 * y : 8 * y + 8] = g


def factor_kernel(gram_ref, p_ref, phat_ref, ph2_ref, linv_ref):
    gp = gram_ref[...]
    n = 64
    left = jnp.concatenate([gp, pltpu.roll(gp, 64, 1)], axis=0)
    row = lax.broadcasted_iota(jnp.int32, (n, 2 * n), 0)
    lane = lax.broadcasted_iota(jnp.int32, (n, 2 * n), 1)
    a = jnp.where(lane < n, left, jnp.where(lane == row + n, 1.0, 0.0))
    for k in range(0, n, 8):
        rows = [a[k + i : k + i + 1, :] for i in range(8)]
        fs = [jnp.broadcast_to(a[:, k + i : k + i + 1], (n, 2 * n)) for i in range(8)]
        for i in range(8):
            d = fs[i][k + i : k + i + 1, :]
            r = lax.rsqrt(d)
            r = r * (1.5 - 0.5 * d * r * r)
            rows[i] = rows[i] * r
            fs[i] = fs[i] * r
            for j in range(i + 1, 8):
                m = fs[i][k + j : k + j + 1, :]
                rows[j] = rows[j] - m * rows[i]
                fs[j] = fs[j] - m * fs[i]
        upd = fs[0] * rows[0]
        for i in range(1, 8):
            upd = upd + fs[i] * rows[i]
        block = jnp.concatenate(rows, axis=0)
        parts = [a[:k]] if k else []
        parts.append(block)
        if k + 8 < n:
            parts.append(a[k + 8 :] - upd[k + 8 :])
        a = jnp.concatenate(parts, axis=0) if len(parts) > 1 else block
    linv = pltpu.roll(a, 64, 1)[:, 0:n]
    linv_ref[...] = linv
    phat = jnp.dot(linv, p_ref[0], precision=HIGH, preferred_element_type=F32)
    phat_ref[...] = phat
    hi = phat.astype(BF)
    ph2_ref[0:64] = hi
    ph2_ref[64:128] = (phat - hi.astype(F32)).astype(BF)


def q_scale_kernel(q0, q1, q2, q3, linv_ref, out_ref):
    s = sum_of((q0, q1, q2, q3)) * (1.0 / 16.0)
    q = jnp.dot(linv_ref[...], s, precision=HIGH, preferred_element_type=F32).astype(BF)
    for k in range(16):
        out_ref[k] = q


def matrix_kernel(at_ref, ga_ref, gb_ref, ea_ref, eb_ref, m_ref):
    at = at_ref[...]
    for j in range(8):
        g, e = (ga_ref[j], ea_ref[j]) if j < 4 else (gb_ref[j - 4], eb_ref[j - 4])
        m_ref[j] = dot(at, g, 1, 0) * (1.0 / 512.0) + e.astype(F32)


def error_half(ph2_ref, q_ref, m_ref, err_hbm, o_buf, sems, base):
    ph = -(ph2_ref[...].T)
    outs = []
    for k in range(4):
        row = block_row(base + k) * 4
        q = jnp.concatenate([q_ref[row + y] for y in range(4)], axis=1)
        q2 = jnp.concatenate([q, q], axis=0)
        o_buf[k] = (m_ref[base + k] + dot(ph, q2, 1, 0)).astype(BF)
        o = pltpu.make_async_copy(o_buf.at[k], err_hbm.at[:, cols(base + k)], sems.at[k])
        o.start()
        outs.append(o)
    return outs


def error_own_kernel(ph2_ref, q_ref, m_ref, err_hbm, qf_ref, o_buf, sems):
    outs = error_half(ph2_ref, q_ref, m_ref, err_hbm, o_buf, sems, 0)
    row = lax.axis_index("x") * 4
    qf_ref[...] = jnp.concatenate([q_ref[row + y] for y in range(4)], axis=1).astype(F32)
    for o in outs:
        o.wait()


def error_sib_kernel(ph2_ref, q_ref, m_ref, _, err_hbm, o_buf, sems):
    for o in error_half(ph2_ref, q_ref, m_ref, err_hbm, o_buf, sems, 4):
        o.wait()


def in_hbm(v):
    return pltpu.with_memory_space_constraint(v, pltpu.HBM)


def shift(v, axis, k):
    n = lax.axis_size(axis)
    return lax.ppermute(v, axis, [(i, (i + k) % n) for i in range(n)])


def swap(v):
    return lax.ppermute(v, "core", [(0, 1), (1, 0)])


def ring(v, axis):
    return [v] + [shift(v, axis, k) for k in (1, 2, 3)]


def exchange(v, axes):
    return lax.all_to_all(v, axes, 0, 0, tiled=True)


def on_device(attn_out, grad_top, branch_grad, error_prev, q_prev):
    act = attn_out.reshape(512, 512)
    top = grad_top.reshape(512, 512)
    br = branch_grad.reshape(512, 512)
    err = error_prev.reshape(512, 4096)
    qt = q_prev[0].T

    qv, top, br, sent = pl.pallas_call(
        load_kernel,
        out_shape=(sds((64, 512), F32), sds((512, 512), BF), sds((512, 512), BF), sds((512, 512), BF)),
        in_specs=[HBM] * 3,
        out_specs=(VMEM,) * 4,
        scratch_shapes=[pltpu.SemaphoreType.DMA((3,))],
        cost_estimate=LIGHT,
        compiler_params=params(4),
        name="load_kernel",
    )(*(in_hbm(v) for v in (qt, top, br)))

    recv = lax.ppermute(sent, "pipe", [(1, 0)])
    qx = ring(qt, "x")
    err, *_ = lax.optimization_barrier((in_hbm(err), *qx[1:]))
    eh, err, act = pl.pallas_call(
        load_error_kernel,
        out_shape=(sds((4, 512, 512), BF), sds((4, 512, 512), BF), sds((512, 512), BF)),
        in_specs=[HBM] * 2,
        out_specs=(VMEM,) * 3,
        scratch_shapes=[pltpu.SemaphoreType.DMA((9,))],
        cost_estimate=LIGHT,
        compiler_params=params(12),
        name="load_error_kernel",
    )(err, in_hbm(act))
    recv, err = lax.optimization_barrier((recv, err))

    grad, u = pl.pallas_call(
        u_kernel,
        out_shape=(sds((512, 512), BF), sds((64, 512), F32)),
        in_specs=[VMEM] * 3,
        out_specs=(VMEM,) * 2,
        cost_estimate=LIGHT,
        compiler_params=params(6),
        name="u_kernel",
    )(top, recv, qv)
    grad_in = pl.pallas_call(
        grad_in_kernel,
        out_shape=sds((512, 512), BF),
        in_specs=[VMEM] * 2,
        out_specs=VMEM,
        cost_estimate=LIGHT,
        compiler_params=params(6),
        name="grad_in_kernel",
    )(grad, br)
    other, grad_in = lax.optimization_barrier((swap(u), grad_in))
    u = u + other
    eh, _ = lax.optimization_barrier((eh, u))
    eh_s = swap(eh)
    us = ring(u, "x")
    eq, eq_sib, act_t = pl.pallas_call(
        eq_kernel,
        out_shape=(sds((64, 512), F32), sds((64, 512), F32), sds((512, 512), BF)),
        in_specs=[VMEM] * 7,
        out_specs=(VMEM,) * 3,
        cost_estimate=LIGHT,
        compiler_params=params(12),
        name="eq_kernel",
    )(qv, *qx[1:], act, err, eh_s)
    eqs = swap(eq_sib)

    part = pl.pallas_call(
        p_kernel,
        out_shape=sds((64, 512), F32),
        in_specs=[VMEM] * 7,
        out_specs=VMEM,
        cost_estimate=LIGHT,
        compiler_params=params(6),
        name="p_kernel",
    )(*us, act, eq, eqs)
    grad, *_ = lax.optimization_barrier((grad, eqs, *us))
    g1 = shift(grad, "x", 1)
    g3 = shift(grad, "x", 3)
    part = pl.pallas_call(
        sum_kernel,
        out_shape=sds((64, 512), F32),
        in_specs=[VMEM] * 4,
        out_specs=VMEM,
        cost_estimate=LIGHT,
        compiler_params=params(4),
        name="sum_kernel",
    )(*ring(part, "y"))

    h1, h3, _ = lax.optimization_barrier((g1, g3, part))
    g2a = shift(h1[:256], "x", 1)
    g2b = shift(h3[256:], "x", 3)
    zs = ring(part, "zhi")
    g2a, g2b, *zs = lax.optimization_barrier((g2a, g2b, *zs))
    pv = pl.pallas_call(
        pv_kernel,
        out_shape=sds((2, 64, 512), F32),
        in_specs=[VMEM] * 5,
        out_specs=VMEM,
        cost_estimate=LIGHT,
        compiler_params=params(4),
        name="pv_kernel",
    )(*zs, act)
    pvs = swap(pv)
    q_own_part = pl.pallas_call(
        q_own_kernel,
        out_shape=sds((4, 64, 512), F32),
        in_specs=[VMEM] * 2,
        out_specs=VMEM,
        cost_estimate=LIGHT,
        compiler_params=params(8),
        name="q_own_kernel",
    )(pv, err)
    chunks, gs = pl.pallas_call(
        q_kernel,
        out_shape=(sds((4, 4, 72, 128), F32), sds((4, 512, 512), BF)),
        in_specs=[VMEM] * 9,
        out_specs=(VMEM, VMEM),
        scratch_shapes=[pltpu.VMEM((32, 128), F32)],
        cost_estimate=LIGHT,
        compiler_params=params(12),
        name="q_kernel",
    )(pv, pvs, q_own_part, eh_s, grad, g1, g2a, g2b, g3)
    gb = swap(gs)
    chunks = exchange(chunks.reshape(16, 72, 128), ("x", "y"))

    q_part, gram = pl.pallas_call(
        chunk_sum_kernel,
        out_shape=(sds((64, 128), F32), sds((32, 128), F32)),
        in_specs=[VMEM],
        out_specs=(VMEM, VMEM),
        cost_estimate=LIGHT,
        compiler_params=params(4),
        name="chunk_sum_kernel",
    )(chunks)
    qs = ring(q_part, "zhi")
    phat, ph2, linv = pl.pallas_call(
        factor_kernel,
        out_shape=(sds((64, 512), F32), sds((128, 512), BF), sds((64, 64), F32)),
        in_specs=[VMEM, VMEM],
        out_specs=(VMEM, VMEM, VMEM),
        cost_estimate=LIGHT,
        compiler_params=params(4),
        name="factor_kernel",
    )(gram, pv)
    act_t, gram = lax.optimization_barrier((act_t, gram))
    matrix = pl.pallas_call(
        matrix_kernel,
        out_shape=sds((8, 512, 512), F32),
        in_specs=[VMEM] * 5,
        out_specs=VMEM,
        cost_estimate=LIGHT,
        compiler_params=params(20),
        name="matrix_kernel",
    )(act_t, gs, gb, err, eh)
    matrix, linv = lax.optimization_barrier((matrix, linv))
    q16 = pl.pallas_call(
        q_scale_kernel,
        out_shape=sds((16, 64, 128), BF),
        in_specs=[VMEM] * 5,
        out_specs=VMEM,
        cost_estimate=LIGHT,
        compiler_params=params(4),
        name="q_scale_kernel",
    )(*qs, linv)
    qfa = exchange(q16, ("x", "y"))
    qfb = swap(qfa)

    scratch = [pltpu.VMEM((4, 512, 512), BF), pltpu.SemaphoreType.DMA((4,))]
    error_next, q_own = pl.pallas_call(
        error_own_kernel,
        out_shape=(sds((512, 4096), BF), sds((64, 512), F32)),
        in_specs=[VMEM] * 3,
        out_specs=(HBM, VMEM),
        scratch_shapes=scratch,
        cost_estimate=LIGHT,
        compiler_params=params(14),
        name="error_own_kernel",
    )(ph2, qfa, matrix)
    error_next = pl.pallas_call(
        error_sib_kernel,
        out_shape=sds((512, 4096), BF),
        in_specs=[VMEM] * 3 + [HBM],
        out_specs=HBM,
        scratch_shapes=scratch,
        input_output_aliases={3: 0},
        cost_estimate=LIGHT,
        compiler_params=params(14),
        name="error_sib_kernel",
    )(ph2, qfb, matrix, error_next)
    return (
        grad_in.reshape(branch_grad.shape),
        error_next.reshape(error_prev.shape),
        phat.T[None],
        q_own.T[None],
    )


def solution(mesh):
    fine = Mesh(mesh.devices.reshape(2, 4, 2, 4, 4), ("pipe", "x", "core", "zhi", "y"))
    tensor = ("x", "core")
    dp = ("zhi", "y")
    return jax.shard_map(
        on_device,
        mesh=fine,
        in_specs=(
            P("pipe", None, dp, tensor),
            P(None, dp, tensor),
            P("pipe", None, dp, tensor),
            P("pipe", dp, tensor, None),
            P("pipe", tensor, None),
        ),
        out_specs=(
            P("pipe", None, dp, tensor),
            P("pipe", dp, tensor, None),
            P("pipe", tensor, None),
            P("pipe", tensor, None),
        ),
        check_vma=False,
    )
```

```python
import jax
import jax.numpy as jnp
from jax import lax
from jax.experimental import pallas as pl
from jax.experimental.pallas import tpu as pltpu
from jax.sharding import Mesh, PartitionSpec as P

BF = jnp.bfloat16
F32 = jnp.float32
HIGH = lax.Precision.HIGHEST
MIB = 1024 * 1024
ANY = pl.BlockSpec(memory_space=pl.ANY)
HBM = pl.BlockSpec(memory_space=pltpu.HBM)
VMEM = pl.BlockSpec(memory_space=pltpu.VMEM)
SMEM = pl.BlockSpec(memory_space=pltpu.SMEM)


LIGHT = pl.CostEstimate(flops=0, transcendentals=0, bytes_accessed=0)


def sds(shape, dtype):
    return jax.ShapeDtypeStruct(shape, dtype)


def params(mib):
    return pltpu.CompilerParams(vmem_limit_bytes=mib * MIB)


def split3(v):
    h = v.astype(BF)
    r = v - h.astype(F32)
    m = r.astype(BF)
    l = (r - m.astype(F32)).astype(BF)
    return jnp.concatenate([h, m, l], axis=0)


def fold3(v):
    n = v.shape[0] // 3
    return v[:n] + (v[n : 2 * n] + v[2 * n :])


def dot(a, b, ca, cb):
    return lax.dot_general(a, b, (((ca,), (cb,)), ((), ())), preferred_element_type=F32)


def u_kernel(top_ref, recv_ref, q_ref, g_ref, u_ref):
    last = lax.axis_index("pipe")

    @pl.when(last == 1)
    def _():
        g_ref[...] = top_ref[...]

    @pl.when(last == 0)
    def _():
        g_ref[...] = recv_ref[...]

    u_ref[...] = fold3(dot(split3(q_ref[...]), g_ref[...], 1, 1))


def grad_in_kernel(g_ref, br_ref, gin_ref):
    gin_ref[...] = (g_ref[...].astype(F32) + br_ref[...].astype(F32)).astype(BF)


def block_row(j):
    return lax.rem(lax.axis_index("x") + 4 - j % 4, 4)


def cols(j, w=512):
    c = lax.axis_index("core")
    owner = block_row(j) * 2 + (c if j < 4 else 1 - c)
    return pl.ds(pl.multiple_of(owner * w, w), w)


def eq_kernel(q0, q1, q2, q3, act_ref, e_ref, es_ref, own_ref, sib_ref, at_ref):
    at_ref[...] = act_ref[...].T
    own = sib = None
    for k, q in enumerate((q0, q1, q2, q3)):
        q3 = split3(q[...])
        a = dot(q3, e_ref[k], 1, 1)
        b = dot(q3, es_ref[k], 1, 1)
        own = a if own is None else own + a
        sib = b if sib is None else sib + b
    own_ref[...] = fold3(own)
    sib_ref[...] = fold3(sib)


def p_kernel(u0, u1, u2, u3, act_ref, eq_ref, eqs_ref, out_ref):
    u = sum_of((u0, u1, u2, u3))
    p = fold3(dot(split3(u), act_ref[...], 1, 0)) * (1.0 / 512.0) + (eq_ref[...] + eqs_ref[...])
    out_ref[...] = p


def sum_of(refs):
    a, b, c, d = refs
    return (a[...] + c[...]) + (b[...] + d[...])


def sum_kernel(a, b, c, d, out_ref):
    out_ref[...] = sum_of((a, b, c, d))


def put_chunks(out_ref, slot, r, gram):
    for y in range(4):
        out_ref[slot, y, 0:64, :] = r[:, y * 128 : (y + 1) * 128]
        out_ref[slot, y, 64:72, :] = gram


def run_copies(pairs, sems):
    cps = [pltpu.make_async_copy(s, d, sems.at[i]) for i, (s, d) in enumerate(pairs)]
    for cp in cps:
        cp.start()
    for cp in cps:
        cp.wait()


def load_kernel(q, top, br, q_v, top_v, br_v, s_v, sems):
    run_copies(((q, q_v), (top, top_v), (br, br_v)), sems)
    s_v[...] = (top_v[...].astype(F32) + br_v[...].astype(F32)).astype(BF)


def load_error_kernel(e, act, eh_v, e_v, act_v, sems):
    pairs = [(e.at[:, cols(4 + k)], eh_v.at[k]) for k in range(4)]
    pairs += [(e.at[:, cols(k)], e_v.at[k]) for k in range(4)]
    run_copies(pairs + [(act, act_v)], sems)


def pv_kernel(z0, z1, z2a, z2b, z3, act_ref, out_ref):
    z2 = jnp.concatenate([z2a[...], z2b[...]], axis=1)
    p = ((z0[...] + z2) + (z1[...] + z3[...])) * (1.0 / 16.0)
    out_ref[0] = p
    out_ref[1] = fold3(dot(split3(p), act_ref[...], 1, 1))


def q_own_kernel(pv_ref, e_ref, out_ref):
    p3 = split3(pv_ref[0])
    for k in range(4):
        out_ref[k] = fold3(dot(p3, e_ref[k], 1, 0))


def q_kernel(pv_ref, pvs_ref, r_ref, es_ref, g0, g1, g2a, g2b, g3, out_ref, gs_ref, gram_scr):
    v3 = split3(pv_ref[1] + pvs_ref[1])
    q3 = split3(pvs_ref[0])

    def gram_of(p3):
        return dot(p3, p3[0:64], 1, 1) + (dot(p3, p3[64:128], 1, 1) + dot(p3, p3[128:192], 1, 1))

    g = fold3(gram_of(split3(pv_ref[0])) + gram_of(q3))
    gram_scr[...] = jnp.concatenate([g[0:32], g[32:64]], axis=1)
    gram = gram_scr[pl.ds(pl.multiple_of(lax.axis_index("y") * 8, 8), 8), :]
    for k, gr in enumerate((g0, g1, None, g3)):
        if k == 2:
            vg = dot(v3[:, 0:256], g2a[...], 1, 0) + dot(v3[:, 256:512], g2b[...], 1, 0)
            gs_ref[k, 0:256] = g2a[...]
            gs_ref[k, 256:512] = g2b[...]
        else:
            vg = dot(v3, gr[...], 1, 0)
            gs_ref[k] = gr[...]
        r = fold3(dot(q3, es_ref[k], 1, 0) + vg * (1.0 / 512.0)) + r_ref[k]
        put_chunks(out_ref, block_row(k), r, gram)


def chunk_sum_kernel(in_ref, q_ref, gram_ref):
    s = in_ref[0, 0:64]
    for k in range(1, 16):
        s = s + in_ref[k, 0:64]
    q_ref[...] = s
    for y in range(4):
        g = (in_ref[y, 64:72] + in_ref[4 + y, 64:72]) + (in_ref[8 + y, 64:72] + in_ref[12 + y, 64:72])
        gram_ref[8 * y : 8 * y + 8] = g


def factor_kernel(gram_ref, p_ref, phat_ref, ph2_ref, linv_ref):
    gp = gram_ref[...]
    n = 64
    left = jnp.concatenate([gp, pltpu.roll(gp, 64, 1)], axis=0)
    row = lax.broadcasted_iota(jnp.int32, (n, 2 * n), 0)
    lane = lax.broadcasted_iota(jnp.int32, (n, 2 * n), 1)
    a = jnp.where(lane < n, left, jnp.where(lane == row + n, 1.0, 0.0))
    for k in range(0, n, 8):
        rows = [a[k + i : k + i + 1, :] for i in range(8)]
        fs = [jnp.broadcast_to(a[:, k + i : k + i + 1], (n, 2 * n)) for i in range(8)]
        for i in range(8):
            d = fs[i][k + i : k + i + 1, :]
            r = lax.rsqrt(d)
            r = r * (1.5 - 0.5 * d * r * r)
            rows[i] = rows[i] * r
            fs[i] = fs[i] * r
            for j in range(i + 1, 8):
                m = fs[i][k + j : k + j + 1, :]
                rows[j] = rows[j] - m * rows[i]
                fs[j] = fs[j] - m * fs[i]
        upd = fs[0] * rows[0]
        for i in range(1, 8):
            upd = upd + fs[i] * rows[i]
        block = jnp.concatenate(rows, axis=0)
        parts = [a[:k]] if k else []
        parts.append(block)
        if k + 8 < n:
            parts.append(a[k + 8 :] - upd[k + 8 :])
        a = jnp.concatenate(parts, axis=0) if len(parts) > 1 else block
    linv = pltpu.roll(a, 64, 1)[:, 0:n]
    linv_ref[...] = linv
    phat = jnp.dot(linv, p_ref[0], precision=HIGH, preferred_element_type=F32)
    phat_ref[...] = phat
    hi = phat.astype(BF)
    ph2_ref[0:64] = hi
    ph2_ref[64:128] = (phat - hi.astype(F32)).astype(BF)


def q_scale_kernel(q0, q1, q2, q3, linv_ref, out_ref):
    s = sum_of((q0, q1, q2, q3)) * (1.0 / 16.0)
    q = jnp.dot(linv_ref[...], s, precision=HIGH, preferred_element_type=F32).astype(BF)
    for k in range(16):
        out_ref[k] = q


def matrix_kernel(at_ref, ga_ref, gb_ref, ea_ref, eb_ref, m_ref):
    at = at_ref[...]
    for j in range(8):
        g, e = (ga_ref[j], ea_ref[j]) if j < 4 else (gb_ref[j - 4], eb_ref[j - 4])
        m_ref[j] = dot(at, g, 1, 0) * (1.0 / 512.0) + e.astype(F32)


def error_half(ph2_ref, q_ref, m_ref, err_hbm, o_buf, sems, base):
    ph = -(ph2_ref[...].T)
    outs = []
    for k in range(4):
        row = block_row(base + k) * 4
        q = jnp.concatenate([q_ref[row + y] for y in range(4)], axis=1)
        q2 = jnp.concatenate([q, q], axis=0)
        o_buf[k] = (m_ref[base + k] + dot(ph, q2, 1, 0)).astype(BF)
        o = pltpu.make_async_copy(o_buf.at[k], err_hbm.at[:, cols(base + k)], sems.at[k])
        o.start()
        outs.append(o)
    return outs


def error_own_kernel(ph2_ref, q_ref, m_ref, err_hbm, qf_ref, o_buf, sems):
    outs = error_half(ph2_ref, q_ref, m_ref, err_hbm, o_buf, sems, 0)
    row = lax.axis_index("x") * 4
    qf_ref[...] = jnp.concatenate([q_ref[row + y] for y in range(4)], axis=1).astype(F32)
    for o in outs:
        o.wait()


def error_sib_kernel(ph2_ref, q_ref, m_ref, _, err_hbm, o_buf, sems):
    for o in error_half(ph2_ref, q_ref, m_ref, err_hbm, o_buf, sems, 4):
        o.wait()


def in_hbm(v):
    return pltpu.with_memory_space_constraint(v, pltpu.HBM)


def shift(v, axis, k):
    n = lax.axis_size(axis)
    return lax.ppermute(v, axis, [(i, (i + k) % n) for i in range(n)])


def swap(v):
    return lax.ppermute(v, "core", [(0, 1), (1, 0)])


def ring(v, axis):
    return [v] + [shift(v, axis, k) for k in (1, 2, 3)]


def exchange(v, axes):
    return lax.all_to_all(v, axes, 0, 0, tiled=True)


def on_device(attn_out, grad_top, branch_grad, error_prev, q_prev):
    act = attn_out.reshape(512, 512)
    top = grad_top.reshape(512, 512)
    br = branch_grad.reshape(512, 512)
    err = error_prev.reshape(512, 4096)
    qt = q_prev[0].T

    qv, top, br, sent = pl.pallas_call(
        load_kernel,
        out_shape=(sds((64, 512), F32), sds((512, 512), BF), sds((512, 512), BF), sds((512, 512), BF)),
        in_specs=[HBM] * 3,
        out_specs=(VMEM,) * 4,
        scratch_shapes=[pltpu.SemaphoreType.DMA((3,))],
        cost_estimate=LIGHT,
        compiler_params=params(4),
        name="load_kernel",
    )(*(in_hbm(v) for v in (qt, top, br)))

    recv = lax.ppermute(sent, "pipe", [(1, 0)])
    qx = ring(qt, "x")
    err, *_ = lax.optimization_barrier((in_hbm(err), *qx[1:]))
    eh, err, act = pl.pallas_call(
        load_error_kernel,
        out_shape=(sds((4, 512, 512), BF), sds((4, 512, 512), BF), sds((512, 512), BF)),
        in_specs=[HBM] * 2,
        out_specs=(VMEM,) * 3,
        scratch_shapes=[pltpu.SemaphoreType.DMA((9,))],
        cost_estimate=LIGHT,
        compiler_params=params(12),
        name="load_error_kernel",
    )(err, in_hbm(act))
    recv, err = lax.optimization_barrier((recv, err))

    grad, u = pl.pallas_call(
        u_kernel,
        out_shape=(sds((512, 512), BF), sds((64, 512), F32)),
        in_specs=[VMEM] * 3,
        out_specs=(VMEM,) * 2,
        cost_estimate=LIGHT,
        compiler_params=params(6),
        name="u_kernel",
    )(top, recv, qv)
    grad_in = pl.pallas_call(
        grad_in_kernel,
        out_shape=sds((512, 512), BF),
        in_specs=[VMEM] * 2,
        out_specs=VMEM,
        cost_estimate=LIGHT,
        compiler_params=params(6),
        name="grad_in_kernel",
    )(grad, br)
    other, grad_in = lax.optimization_barrier((swap(u), grad_in))
    u = u + other
    eh, _ = lax.optimization_barrier((eh, u))
    eh_s = swap(eh)
    us = ring(u, "x")
    eq, eq_sib, act_t = pl.pallas_call(
        eq_kernel,
        out_shape=(sds((64, 512), F32), sds((64, 512), F32), sds((512, 512), BF)),
        in_specs=[VMEM] * 7,
        out_specs=(VMEM,) * 3,
        cost_estimate=LIGHT,
        compiler_params=params(12),
        name="eq_kernel",
    )(qv, *qx[1:], act, err, eh_s)
    eqs = swap(eq_sib)

    part = pl.pallas_call(
        p_kernel,
        out_shape=sds((64, 512), F32),
        in_specs=[VMEM] * 7,
        out_specs=VMEM,
        cost_estimate=LIGHT,
        compiler_params=params(6),
        name="p_kernel",
    )(*us, act, eq, eqs)
    ys = ring(part, "y")
    grad, *_ = lax.optimization_barrier((grad, eqs, *us))
    g1 = shift(grad, "x", 1)
    g3 = shift(grad, "x", 3)
    part = pl.pallas_call(
        sum_kernel,
        out_shape=sds((64, 512), F32),
        in_specs=[VMEM] * 4,
        out_specs=VMEM,
        cost_estimate=LIGHT,
        compiler_params=params(4),
        name="sum_kernel",
    )(*ys)

    z1 = shift(part, "zhi", 1)
    z3 = shift(part, "zhi", 3)
    h1, h3, *_ = lax.optimization_barrier((g1, g3, z1, z3))
    g2a = shift(h1[:256], "x", 1)
    g2b = shift(h3[256:], "x", 3)
    z2a = shift(z1[:, :256], "zhi", 1)
    z2b = shift(z3[:, 256:], "zhi", 3)
    g2a, g2b, z2a, z2b = lax.optimization_barrier((g2a, g2b, z2a, z2b))
    pv = pl.pallas_call(
        pv_kernel,
        out_shape=sds((2, 64, 512), F32),
        in_specs=[VMEM] * 6,
        out_specs=VMEM,
        cost_estimate=LIGHT,
        compiler_params=params(4),
        name="pv_kernel",
    )(part, z1, z2a, z2b, z3, act)
    pvs = swap(pv)
    q_own_part = pl.pallas_call(
        q_own_kernel,
        out_shape=sds((4, 64, 512), F32),
        in_specs=[VMEM] * 2,
        out_specs=VMEM,
        cost_estimate=LIGHT,
        compiler_params=params(8),
        name="q_own_kernel",
    )(pv, err)
    chunks, gs = pl.pallas_call(
        q_kernel,
        out_shape=(sds((4, 4, 72, 128), F32), sds((4, 512, 512), BF)),
        in_specs=[VMEM] * 9,
        out_specs=(VMEM, VMEM),
        scratch_shapes=[pltpu.VMEM((32, 128), F32)],
        cost_estimate=LIGHT,
        compiler_params=params(12),
        name="q_kernel",
    )(pv, pvs, q_own_part, eh_s, grad, g1, g2a, g2b, g3)
    gb = swap(gs)
    chunks = exchange(chunks.reshape(16, 72, 128), ("x", "y"))

    q_part, gram = pl.pallas_call(
        chunk_sum_kernel,
        out_shape=(sds((64, 128), F32), sds((32, 128), F32)),
        in_specs=[VMEM],
        out_specs=(VMEM, VMEM),
        cost_estimate=LIGHT,
        compiler_params=params(4),
        name="chunk_sum_kernel",
    )(chunks)
    qs = ring(q_part, "zhi")
    phat, ph2, linv = pl.pallas_call(
        factor_kernel,
        out_shape=(sds((64, 512), F32), sds((128, 512), BF), sds((64, 64), F32)),
        in_specs=[VMEM, VMEM],
        out_specs=(VMEM, VMEM, VMEM),
        cost_estimate=LIGHT,
        compiler_params=params(4),
        name="factor_kernel",
    )(gram, pv)
    act_t, gram = lax.optimization_barrier((act_t, gram))
    matrix = pl.pallas_call(
        matrix_kernel,
        out_shape=sds((8, 512, 512), F32),
        in_specs=[VMEM] * 5,
        out_specs=VMEM,
        cost_estimate=LIGHT,
        compiler_params=params(20),
        name="matrix_kernel",
    )(act_t, gs, gb, err, eh)
    matrix, linv = lax.optimization_barrier((matrix, linv))
    q16 = pl.pallas_call(
        q_scale_kernel,
        out_shape=sds((16, 64, 128), BF),
        in_specs=[VMEM] * 5,
        out_specs=VMEM,
        cost_estimate=LIGHT,
        compiler_params=params(4),
        name="q_scale_kernel",
    )(*qs, linv)
    qfa = exchange(q16, ("x", "y"))
    qfb = swap(qfa)

    scratch = [pltpu.VMEM((4, 512, 512), BF), pltpu.SemaphoreType.DMA((4,))]
    error_next, q_own = pl.pallas_call(
        error_own_kernel,
        out_shape=(sds((512, 4096), BF), sds((64, 512), F32)),
        in_specs=[VMEM] * 3,
        out_specs=(HBM, VMEM),
        scratch_shapes=scratch,
        cost_estimate=LIGHT,
        compiler_params=params(14),
        name="error_own_kernel",
    )(ph2, qfa, matrix)
    error_next = pl.pallas_call(
        error_sib_kernel,
        out_shape=sds((512, 4096), BF),
        in_specs=[VMEM] * 3 + [HBM],
        out_specs=HBM,
        scratch_shapes=scratch,
        input_output_aliases={3: 0},
        cost_estimate=LIGHT,
        compiler_params=params(14),
        name="error_sib_kernel",
    )(ph2, qfb, matrix, error_next)
    return (
        grad_in.reshape(branch_grad.shape),
        error_next.reshape(error_prev.shape),
        phat.T[None],
        q_own.T[None],
    )


def solution(mesh):
    fine = Mesh(mesh.devices.reshape(2, 4, 2, 4, 4), ("pipe", "x", "core", "zhi", "y"))
    tensor = ("x", "core")
    dp = ("zhi", "y")
    return jax.shard_map(
        on_device,
        mesh=fine,
        in_specs=(
            P("pipe", None, dp, tensor),
            P(None, dp, tensor),
            P("pipe", None, dp, tensor),
            P("pipe", dp, tensor, None),
            P("pipe", tensor, None),
        ),
        out_specs=(
            P("pipe", None, dp, tensor),
            P("pipe", dp, tensor, None),
            P("pipe", tensor, None),
            P("pipe", tensor, None),
        ),
        check_vma=False,
    )
```

```python
import jax
import jax.numpy as jnp
from jax import lax
from jax.experimental import pallas as pl
from jax.experimental.pallas import tpu as pltpu
from jax.sharding import Mesh, PartitionSpec as P

BF = jnp.bfloat16
F32 = jnp.float32
HIGH = lax.Precision.HIGHEST
MIB = 1024 * 1024
ANY = pl.BlockSpec(memory_space=pl.ANY)
HBM = pl.BlockSpec(memory_space=pltpu.HBM)
VMEM = pl.BlockSpec(memory_space=pltpu.VMEM)
SMEM = pl.BlockSpec(memory_space=pltpu.SMEM)


LIGHT = pl.CostEstimate(flops=0, transcendentals=0, bytes_accessed=0)


def sds(shape, dtype):
    return jax.ShapeDtypeStruct(shape, dtype)


def params(mib):
    return pltpu.CompilerParams(vmem_limit_bytes=mib * MIB)


def split3(v):
    h = v.astype(BF)
    r = v - h.astype(F32)
    m = r.astype(BF)
    l = (r - m.astype(F32)).astype(BF)
    return jnp.concatenate([h, m, l], axis=0)


def fold3(v):
    n = v.shape[0] // 3
    return v[:n] + (v[n : 2 * n] + v[2 * n :])


def dot(a, b, ca, cb):
    return lax.dot_general(a, b, (((ca,), (cb,)), ((), ())), preferred_element_type=F32)


def u_kernel(top_ref, recv_ref, q_ref, g_ref, u_ref):
    last = lax.axis_index("pipe")

    @pl.when(last == 1)
    def _():
        g_ref[...] = top_ref[...]

    @pl.when(last == 0)
    def _():
        g_ref[...] = recv_ref[...]

    u_ref[...] = fold3(dot(split3(q_ref[...]), g_ref[...], 1, 1))


def grad_in_kernel(g_ref, br_ref, gin_ref):
    gin_ref[...] = (g_ref[...].astype(F32) + br_ref[...].astype(F32)).astype(BF)


def block_row(j):
    return lax.rem(lax.axis_index("x") + 4 - j % 4, 4)


def cols(j, w=512):
    c = lax.axis_index("core")
    owner = block_row(j) * 2 + (c if j < 4 else 1 - c)
    return pl.ds(pl.multiple_of(owner * w, w), w)


def eq_kernel(q0, q1, q2, q3, act_ref, e_ref, es_ref, own_ref, sib_ref, at_ref):
    at_ref[...] = act_ref[...].T
    own = sib = None
    for k, q in enumerate((q0, q1, q2, q3)):
        q3 = split3(q[...])
        a = dot(q3, e_ref[k], 1, 1)
        b = dot(q3, es_ref[k], 1, 1)
        own = a if own is None else own + a
        sib = b if sib is None else sib + b
    own_ref[...] = fold3(own)
    sib_ref[...] = fold3(sib)


def p_kernel(u0, u1, u2, u3, act_ref, eq_ref, eqs_ref, out_ref):
    u = sum_of((u0, u1, u2, u3))
    p = fold3(dot(split3(u), act_ref[...], 1, 0)) * (1.0 / 512.0) + (eq_ref[...] + eqs_ref[...])
    out_ref[...] = p


def sum_of(refs):
    a, b, c, d = refs
    return (a[...] + c[...]) + (b[...] + d[...])


def sum_kernel(a, b, c, d, out_ref):
    out_ref[...] = sum_of((a, b, c, d))


def put_chunks(out_ref, slot, r, gram):
    for y in range(4):
        out_ref[slot, y, 0:64, :] = r[:, y * 128 : (y + 1) * 128]
        out_ref[slot, y, 64:72, :] = gram


def run_copies(pairs, sems):
    cps = [pltpu.make_async_copy(s, d, sems.at[i]) for i, (s, d) in enumerate(pairs)]
    for cp in cps:
        cp.start()
    for cp in cps:
        cp.wait()


def load_kernel(q, top, br, q_v, top_v, br_v, s_v, sems):
    run_copies(((q, q_v), (top, top_v), (br, br_v)), sems)
    s_v[...] = (top_v[...].astype(F32) + br_v[...].astype(F32)).astype(BF)


def load_error_kernel(e, act, eh_v, e_v, act_v, sems):
    pairs = [(e.at[:, cols(4 + k)], eh_v.at[k]) for k in range(4)]
    pairs += [(e.at[:, cols(k)], e_v.at[k]) for k in range(4)]
    run_copies(pairs + [(act, act_v)], sems)


def pv_kernel(z0, z1, z2a, z2b, z3, act_ref, p_ref, v_ref):
    z2 = jnp.concatenate([z2a[...], z2b[...]], axis=1)
    p = ((z0[...] + z2) + (z1[...] + z3[...])) * (1.0 / 16.0)
    p_ref[...] = p
    v_ref[...] = fold3(dot(split3(p), act_ref[...], 1, 1))


def q_own_kernel(p_ref, e_ref, out_ref):
    p3 = split3(p_ref[...])
    for k in range(4):
        out_ref[k] = fold3(dot(p3, e_ref[k], 1, 0))


def q_kernel(p_ref, v_ref, ps_ref, vs_ref, r_ref, es_ref, g0, g1, g2a, g2b, g3, out_ref, gs_ref, gram_scr):
    v3 = split3(v_ref[...] + vs_ref[...])
    q3 = split3(ps_ref[...])

    def gram_of(p3):
        return dot(p3, p3[0:64], 1, 1) + (dot(p3, p3[64:128], 1, 1) + dot(p3, p3[128:192], 1, 1))

    g = fold3(gram_of(split3(p_ref[...])) + gram_of(q3))
    gram_scr[...] = jnp.concatenate([g[0:32], g[32:64]], axis=1)
    gram = gram_scr[pl.ds(pl.multiple_of(lax.axis_index("y") * 8, 8), 8), :]
    for k, gr in enumerate((g0, g1, None, g3)):
        if k == 2:
            vg = dot(v3[:, 0:256], g2a[...], 1, 0) + dot(v3[:, 256:512], g2b[...], 1, 0)
            gs_ref[k, 0:256] = g2a[...]
            gs_ref[k, 256:512] = g2b[...]
        else:
            vg = dot(v3, gr[...], 1, 0)
            gs_ref[k] = gr[...]
        r = fold3(dot(q3, es_ref[k], 1, 0) + vg * (1.0 / 512.0)) + r_ref[k]
        put_chunks(out_ref, block_row(k), r, gram)


def chunk_sum_kernel(in_ref, q_ref, gram_ref):
    s = in_ref[0, 0:64]
    for k in range(1, 16):
        s = s + in_ref[k, 0:64]
    q_ref[...] = s
    for y in range(4):
        g = (in_ref[y, 64:72] + in_ref[4 + y, 64:72]) + (in_ref[8 + y, 64:72] + in_ref[12 + y, 64:72])
        gram_ref[8 * y : 8 * y + 8] = g


def factor_kernel(gram_ref, p_ref, phat_ref, ph2_ref, linv_ref):
    gp = gram_ref[...]
    n = 64
    left = jnp.concatenate([gp, pltpu.roll(gp, 64, 1)], axis=0)
    row = lax.broadcasted_iota(jnp.int32, (n, 2 * n), 0)
    lane = lax.broadcasted_iota(jnp.int32, (n, 2 * n), 1)
    a = jnp.where(lane < n, left, jnp.where(lane == row + n, 1.0, 0.0))
    for k in range(0, n, 8):
        rows = [a[k + i : k + i + 1, :] for i in range(8)]
        fs = [jnp.broadcast_to(a[:, k + i : k + i + 1], (n, 2 * n)) for i in range(8)]
        for i in range(8):
            d = fs[i][k + i : k + i + 1, :]
            r = lax.rsqrt(d)
            r = r * (1.5 - 0.5 * d * r * r)
            rows[i] = rows[i] * r
            fs[i] = fs[i] * r
            for j in range(i + 1, 8):
                m = fs[i][k + j : k + j + 1, :]
                rows[j] = rows[j] - m * rows[i]
                fs[j] = fs[j] - m * fs[i]
        upd = fs[0] * rows[0]
        for i in range(1, 8):
            upd = upd + fs[i] * rows[i]
        block = jnp.concatenate(rows, axis=0)
        parts = [a[:k]] if k else []
        parts.append(block)
        if k + 8 < n:
            parts.append(a[k + 8 :] - upd[k + 8 :])
        a = jnp.concatenate(parts, axis=0) if len(parts) > 1 else block
    linv = pltpu.roll(a, 64, 1)[:, 0:n]
    linv_ref[...] = linv
    phat = jnp.dot(linv, p_ref[...], precision=HIGH, preferred_element_type=F32)
    phat_ref[...] = phat
    hi = phat.astype(BF)
    ph2_ref[0:64] = hi
    ph2_ref[64:128] = (phat - hi.astype(F32)).astype(BF)


def q_scale_kernel(q0, q1, q2, q3, linv_ref, out_ref):
    s = sum_of((q0, q1, q2, q3)) * (1.0 / 16.0)
    q = jnp.dot(linv_ref[...], s, precision=HIGH, preferred_element_type=F32).astype(BF)
    for k in range(16):
        out_ref[k] = q


def matrix_kernel(at_ref, ga_ref, gb_ref, ea_ref, eb_ref, m_ref):
    at = at_ref[...]
    for j in range(8):
        g, e = (ga_ref[j], ea_ref[j]) if j < 4 else (gb_ref[j - 4], eb_ref[j - 4])
        m_ref[j] = dot(at, g, 1, 0) * (1.0 / 512.0) + e.astype(F32)


def error_half(ph2_ref, q_ref, m_ref, err_hbm, o_buf, sems, base):
    ph = -(ph2_ref[...].T)
    outs = []
    for k in range(4):
        row = block_row(base + k) * 4
        q = jnp.concatenate([q_ref[row + y] for y in range(4)], axis=1)
        q2 = jnp.concatenate([q, q], axis=0)
        o_buf[k] = (m_ref[base + k] + dot(ph, q2, 1, 0)).astype(BF)
        o = pltpu.make_async_copy(o_buf.at[k], err_hbm.at[:, cols(base + k)], sems.at[k])
        o.start()
        outs.append(o)
    return outs


def error_own_kernel(ph2_ref, q_ref, m_ref, err_hbm, qf_ref, o_buf, sems):
    outs = error_half(ph2_ref, q_ref, m_ref, err_hbm, o_buf, sems, 0)
    row = lax.axis_index("x") * 4
    qf_ref[...] = jnp.concatenate([q_ref[row + y] for y in range(4)], axis=1).astype(F32)
    for o in outs:
        o.wait()


def error_sib_kernel(ph2_ref, q_ref, m_ref, _, err_hbm, o_buf, sems):
    for o in error_half(ph2_ref, q_ref, m_ref, err_hbm, o_buf, sems, 4):
        o.wait()


def in_hbm(v):
    return pltpu.with_memory_space_constraint(v, pltpu.HBM)


def shift(v, axis, k):
    n = lax.axis_size(axis)
    return lax.ppermute(v, axis, [(i, (i + k) % n) for i in range(n)])


def swap(v):
    return lax.ppermute(v, "core", [(0, 1), (1, 0)])


def ring(v, axis):
    return [v] + [shift(v, axis, k) for k in (1, 2, 3)]


def exchange(v, axes):
    return lax.all_to_all(v, axes, 0, 0, tiled=True)


def on_device(attn_out, grad_top, branch_grad, error_prev, q_prev):
    act = attn_out.reshape(512, 512)
    top = grad_top.reshape(512, 512)
    br = branch_grad.reshape(512, 512)
    err = error_prev.reshape(512, 4096)
    qt = q_prev[0].T

    qv, top, br, sent = pl.pallas_call(
        load_kernel,
        out_shape=(sds((64, 512), F32), sds((512, 512), BF), sds((512, 512), BF), sds((512, 512), BF)),
        in_specs=[HBM] * 3,
        out_specs=(VMEM,) * 4,
        scratch_shapes=[pltpu.SemaphoreType.DMA((3,))],
        cost_estimate=LIGHT,
        compiler_params=params(4),
        name="load_kernel",
    )(*(in_hbm(v) for v in (qt, top, br)))

    recv = lax.ppermute(sent, "pipe", [(1, 0)])
    qx = ring(qt, "x")
    err, *_ = lax.optimization_barrier((in_hbm(err), *qx[1:]))
    eh, err, act = pl.pallas_call(
        load_error_kernel,
        out_shape=(sds((4, 512, 512), BF), sds((4, 512, 512), BF), sds((512, 512), BF)),
        in_specs=[HBM] * 2,
        out_specs=(VMEM,) * 3,
        scratch_shapes=[pltpu.SemaphoreType.DMA((9,))],
        cost_estimate=LIGHT,
        compiler_params=params(12),
        name="load_error_kernel",
    )(err, in_hbm(act))
    recv, err = lax.optimization_barrier((recv, err))

    grad, u = pl.pallas_call(
        u_kernel,
        out_shape=(sds((512, 512), BF), sds((64, 512), F32)),
        in_specs=[VMEM] * 3,
        out_specs=(VMEM,) * 2,
        cost_estimate=LIGHT,
        compiler_params=params(6),
        name="u_kernel",
    )(top, recv, qv)
    grad_in = pl.pallas_call(
        grad_in_kernel,
        out_shape=sds((512, 512), BF),
        in_specs=[VMEM] * 2,
        out_specs=VMEM,
        cost_estimate=LIGHT,
        compiler_params=params(6),
        name="grad_in_kernel",
    )(grad, br)
    other, grad_in = lax.optimization_barrier((swap(u), grad_in))
    u = u + other
    eh, _ = lax.optimization_barrier((eh, u))
    eh_s = swap(eh)
    us = ring(u, "x")
    eq, eq_sib, act_t = pl.pallas_call(
        eq_kernel,
        out_shape=(sds((64, 512), F32), sds((64, 512), F32), sds((512, 512), BF)),
        in_specs=[VMEM] * 7,
        out_specs=(VMEM,) * 3,
        cost_estimate=LIGHT,
        compiler_params=params(12),
        name="eq_kernel",
    )(qv, *qx[1:], act, err, eh_s)
    eqs = swap(eq_sib)

    part = pl.pallas_call(
        p_kernel,
        out_shape=sds((64, 512), F32),
        in_specs=[VMEM] * 7,
        out_specs=VMEM,
        cost_estimate=LIGHT,
        compiler_params=params(6),
        name="p_kernel",
    )(*us, act, eq, eqs)
    ys = ring(part, "y")
    grad, *_ = lax.optimization_barrier((grad, eqs, *us))
    g1 = shift(grad, "x", 1)
    g3 = shift(grad, "x", 3)
    part = pl.pallas_call(
        sum_kernel,
        out_shape=sds((64, 512), F32),
        in_specs=[VMEM] * 4,
        out_specs=VMEM,
        cost_estimate=LIGHT,
        compiler_params=params(4),
        name="sum_kernel",
    )(*ys)

    z1 = shift(part, "zhi", 1)
    z3 = shift(part, "zhi", 3)
    h1, h3, *_ = lax.optimization_barrier((g1, g3, z3))
    g2a = shift(h1[:256], "x", 1)
    g2b = shift(h3[256:], "x", 3)
    z2a = shift(z1[:, :256], "zhi", 1)
    z2b = shift(z3[:, 256:], "zhi", 3)
    p, v = pl.pallas_call(
        pv_kernel,
        out_shape=(sds((64, 512), F32), sds((64, 512), F32)),
        in_specs=[VMEM] * 6,
        out_specs=(VMEM, VMEM),
        cost_estimate=LIGHT,
        compiler_params=params(4),
        name="pv_kernel",
    )(part, z1, z2a, z2b, z3, act)
    ps = swap(p)
    vs = swap(v)
    q_own_part = pl.pallas_call(
        q_own_kernel,
        out_shape=sds((4, 64, 512), F32),
        in_specs=[VMEM] * 2,
        out_specs=VMEM,
        cost_estimate=LIGHT,
        compiler_params=params(8),
        name="q_own_kernel",
    )(p, err)
    chunks, gs = pl.pallas_call(
        q_kernel,
        out_shape=(sds((4, 4, 72, 128), F32), sds((4, 512, 512), BF)),
        in_specs=[VMEM] * 11,
        out_specs=(VMEM, VMEM),
        scratch_shapes=[pltpu.VMEM((32, 128), F32)],
        cost_estimate=LIGHT,
        compiler_params=params(12),
        name="q_kernel",
    )(p, v, ps, vs, q_own_part, eh_s, grad, g1, g2a, g2b, g3)
    gb = swap(gs)
    chunks = exchange(chunks.reshape(16, 72, 128), ("x", "y"))

    q_part, gram = pl.pallas_call(
        chunk_sum_kernel,
        out_shape=(sds((64, 128), F32), sds((32, 128), F32)),
        in_specs=[VMEM],
        out_specs=(VMEM, VMEM),
        cost_estimate=LIGHT,
        compiler_params=params(4),
        name="chunk_sum_kernel",
    )(chunks)
    qs = ring(q_part, "zhi")
    phat, ph2, linv = pl.pallas_call(
        factor_kernel,
        out_shape=(sds((64, 512), F32), sds((128, 512), BF), sds((64, 64), F32)),
        in_specs=[VMEM, VMEM],
        out_specs=(VMEM, VMEM, VMEM),
        cost_estimate=LIGHT,
        compiler_params=params(4),
        name="factor_kernel",
    )(gram, p)
    act_t, gram = lax.optimization_barrier((act_t, gram))
    matrix = pl.pallas_call(
        matrix_kernel,
        out_shape=sds((8, 512, 512), F32),
        in_specs=[VMEM] * 5,
        out_specs=VMEM,
        cost_estimate=LIGHT,
        compiler_params=params(20),
        name="matrix_kernel",
    )(act_t, gs, gb, err, eh)
    matrix, linv = lax.optimization_barrier((matrix, linv))
    q16 = pl.pallas_call(
        q_scale_kernel,
        out_shape=sds((16, 64, 128), BF),
        in_specs=[VMEM] * 5,
        out_specs=VMEM,
        cost_estimate=LIGHT,
        compiler_params=params(4),
        name="q_scale_kernel",
    )(*qs, linv)
    qfa = exchange(q16, ("x", "y"))
    qfb = swap(qfa)

    scratch = [pltpu.VMEM((4, 512, 512), BF), pltpu.SemaphoreType.DMA((4,))]
    error_next, q_own = pl.pallas_call(
        error_own_kernel,
        out_shape=(sds((512, 4096), BF), sds((64, 512), F32)),
        in_specs=[VMEM] * 3,
        out_specs=(HBM, VMEM),
        scratch_shapes=scratch,
        cost_estimate=LIGHT,
        compiler_params=params(14),
        name="error_own_kernel",
    )(ph2, qfa, matrix)
    error_next = pl.pallas_call(
        error_sib_kernel,
        out_shape=sds((512, 4096), BF),
        in_specs=[VMEM] * 3 + [HBM],
        out_specs=HBM,
        scratch_shapes=scratch,
        input_output_aliases={3: 0},
        cost_estimate=LIGHT,
        compiler_params=params(14),
        name="error_sib_kernel",
    )(ph2, qfb, matrix, error_next)
    return (
        grad_in.reshape(branch_grad.shape),
        error_next.reshape(error_prev.shape),
        phat.T[None],
        q_own.T[None],
    )


def solution(mesh):
    fine = Mesh(mesh.devices.reshape(2, 4, 2, 4, 4), ("pipe", "x", "core", "zhi", "y"))
    tensor = ("x", "core")
    dp = ("zhi", "y")
    return jax.shard_map(
        on_device,
        mesh=fine,
        in_specs=(
            P("pipe", None, dp, tensor),
            P(None, dp, tensor),
            P("pipe", None, dp, tensor),
            P("pipe", dp, tensor, None),
            P("pipe", tensor, None),
        ),
        out_specs=(
            P("pipe", None, dp, tensor),
            P("pipe", dp, tensor, None),
            P("pipe", tensor, None),
            P("pipe", tensor, None),
        ),
        check_vma=False,
    )
```

```python
import jax
import jax.numpy as jnp
from jax import lax
from jax.experimental import pallas as pl
from jax.experimental.pallas import tpu as pltpu
from jax.sharding import Mesh, PartitionSpec as P

BF = jnp.bfloat16
F32 = jnp.float32
HIGH = lax.Precision.HIGHEST
MIB = 1024 * 1024
ANY = pl.BlockSpec(memory_space=pl.ANY)
HBM = pl.BlockSpec(memory_space=pltpu.HBM)
VMEM = pl.BlockSpec(memory_space=pltpu.VMEM)
SMEM = pl.BlockSpec(memory_space=pltpu.SMEM)


LIGHT = pl.CostEstimate(flops=0, transcendentals=0, bytes_accessed=0)


def sds(shape, dtype):
    return jax.ShapeDtypeStruct(shape, dtype)


def params(mib):
    return pltpu.CompilerParams(vmem_limit_bytes=mib * MIB)


def split3(v):
    h = v.astype(BF)
    r = v - h.astype(F32)
    m = r.astype(BF)
    l = (r - m.astype(F32)).astype(BF)
    return jnp.concatenate([h, m, l], axis=0)


def fold3(v):
    n = v.shape[0] // 3
    return v[:n] + (v[n : 2 * n] + v[2 * n :])


def dot(a, b, ca, cb):
    return lax.dot_general(a, b, (((ca,), (cb,)), ((), ())), preferred_element_type=F32)


def u_kernel(top_ref, recv_ref, q_ref, g_ref, u_ref):
    last = lax.axis_index("pipe")

    @pl.when(last == 1)
    def _():
        g_ref[...] = top_ref[...]

    @pl.when(last == 0)
    def _():
        g_ref[...] = recv_ref[...]

    u_ref[...] = fold3(dot(split3(q_ref[...]), g_ref[...], 1, 1))


def grad_in_kernel(g_ref, br_ref, gin_ref):
    gin_ref[...] = (g_ref[...].astype(F32) + br_ref[...].astype(F32)).astype(BF)


def block_row(j):
    return lax.rem(lax.axis_index("x") + 4 - j % 4, 4)


def cols(j, w=512):
    c = lax.axis_index("core")
    owner = block_row(j) * 2 + (c if j < 4 else 1 - c)
    return pl.ds(pl.multiple_of(owner * w, w), w)


def eq_kernel(q0, q1, q2, q3, act_ref, e_ref, es_ref, own_ref, sib_ref, at_ref):
    at_ref[...] = act_ref[...].T
    own = sib = None
    for k, q in enumerate((q0, q1, q2, q3)):
        q3 = split3(q[...])
        a = dot(q3, e_ref[k], 1, 1)
        b = dot(q3, es_ref[k], 1, 1)
        own = a if own is None else own + a
        sib = b if sib is None else sib + b
    own_ref[...] = fold3(own)
    sib_ref[...] = fold3(sib)


def p_kernel(u0, u1, u2, u3, act_ref, eq_ref, eqs_ref, out_ref):
    u = sum_of((u0, u1, u2, u3))
    p = fold3(dot(split3(u), act_ref[...], 1, 0)) * (1.0 / 512.0) + (eq_ref[...] + eqs_ref[...])
    out_ref[...] = p


def sum_of(refs):
    a, b, c, d = refs
    return (a[...] + c[...]) + (b[...] + d[...])


def sum_kernel(a, b, c, d, lo_ref, hi_ref):
    s = sum_of((a, b, c, d))
    lo_ref[...] = s[:, 0:256]
    hi_ref[...] = s[:, 256:512]


def add_kernel(a, b, c, d, ab_ref, cd_ref):
    ab_ref[...] = a[...] + b[...]
    cd_ref[...] = c[...] + d[...]


def put_chunks(out_ref, slot, r, gram):
    for y in range(4):
        out_ref[slot, y, 0:64, :] = r[:, y * 128 : (y + 1) * 128]
        out_ref[slot, y, 64:72, :] = gram


def run_copies(pairs, sems):
    cps = [pltpu.make_async_copy(s, d, sems.at[i]) for i, (s, d) in enumerate(pairs)]
    for cp in cps:
        cp.start()
    for cp in cps:
        cp.wait()


def load_kernel(q, top, br, q_v, top_v, br_v, s_v, sems):
    run_copies(((q, q_v), (top, top_v), (br, br_v)), sems)
    s_v[...] = (top_v[...].astype(F32) + br_v[...].astype(F32)).astype(BF)


def load_error_kernel(e, act, eh_v, e_v, act_v, sems):
    pairs = [(e.at[:, cols(4 + k)], eh_v.at[k]) for k in range(4)]
    pairs += [(e.at[:, cols(k)], e_v.at[k]) for k in range(4)]
    run_copies(pairs + [(act, act_v)], sems)


def pv_kernel(lo, lo_far, hi, hi_far, act_ref, p_ref, v_ref):
    p = jnp.concatenate([lo[...] + lo_far[...], hi[...] + hi_far[...]], axis=1) * (1.0 / 16.0)
    p_ref[...] = p
    v_ref[...] = fold3(dot(split3(p), act_ref[...], 1, 1))


def q_own_kernel(p_ref, e_ref, out_ref):
    p3 = split3(p_ref[...])
    for k in range(4):
        out_ref[k] = fold3(dot(p3, e_ref[k], 1, 0))


def q_kernel(p_ref, v_ref, ps_ref, vs_ref, r_ref, es_ref, g0, g1, g2a, g2b, g3, out_ref, gs_ref, gram_scr):
    v3 = split3(v_ref[...] + vs_ref[...])
    q3 = split3(ps_ref[...])

    def gram_of(p3):
        return dot(p3, p3[0:64], 1, 1) + (dot(p3, p3[64:128], 1, 1) + dot(p3, p3[128:192], 1, 1))

    g = fold3(gram_of(split3(p_ref[...])) + gram_of(q3))
    gram_scr[...] = jnp.concatenate([g[0:32], g[32:64]], axis=1)
    gram = gram_scr[pl.ds(pl.multiple_of(lax.axis_index("y") * 8, 8), 8), :]
    for k, gr in enumerate((g0, g1, None, g3)):
        if k == 2:
            vg = dot(v3[:, 0:256], g2a[...], 1, 0) + dot(v3[:, 256:512], g2b[...], 1, 0)
            gs_ref[k, 0:256] = g2a[...]
            gs_ref[k, 256:512] = g2b[...]
        else:
            vg = dot(v3, gr[...], 1, 0)
            gs_ref[k] = gr[...]
        r = fold3(dot(q3, es_ref[k], 1, 0) + vg * (1.0 / 512.0)) + r_ref[k]
        put_chunks(out_ref, block_row(k), r, gram)


def chunk_sum_kernel(in_ref, q_ref, gram_ref):
    s = in_ref[0, 0:64]
    for k in range(1, 16):
        s = s + in_ref[k, 0:64]
    q_ref[...] = s
    for y in range(4):
        g = (in_ref[y, 64:72] + in_ref[4 + y, 64:72]) + (in_ref[8 + y, 64:72] + in_ref[12 + y, 64:72])
        gram_ref[8 * y : 8 * y + 8] = g


def factor_kernel(gram_ref, p_ref, phat_ref, ph2_ref, linv_ref):
    gp = gram_ref[...]
    n = 64
    left = jnp.concatenate([gp, pltpu.roll(gp, 64, 1)], axis=0)
    row = lax.broadcasted_iota(jnp.int32, (n, 2 * n), 0)
    lane = lax.broadcasted_iota(jnp.int32, (n, 2 * n), 1)
    a = jnp.where(lane < n, left, jnp.where(lane == row + n, 1.0, 0.0))
    for k in range(0, n, 8):
        rows = [a[k + i : k + i + 1, :] for i in range(8)]
        fs = [jnp.broadcast_to(a[:, k + i : k + i + 1], (n, 2 * n)) for i in range(8)]
        for i in range(8):
            d = fs[i][k + i : k + i + 1, :]
            r = lax.rsqrt(d)
            r = r * (1.5 - 0.5 * d * r * r)
            rows[i] = rows[i] * r
            fs[i] = fs[i] * r
            for j in range(i + 1, 8):
                m = fs[i][k + j : k + j + 1, :]
                rows[j] = rows[j] - m * rows[i]
                fs[j] = fs[j] - m * fs[i]
        upd = fs[0] * rows[0]
        for i in range(1, 8):
            upd = upd + fs[i] * rows[i]
        block = jnp.concatenate(rows, axis=0)
        parts = [a[:k]] if k else []
        parts.append(block)
        if k + 8 < n:
            parts.append(a[k + 8 :] - upd[k + 8 :])
        a = jnp.concatenate(parts, axis=0) if len(parts) > 1 else block
    linv = pltpu.roll(a, 64, 1)[:, 0:n]
    linv_ref[...] = linv
    phat = jnp.dot(linv, p_ref[...], precision=HIGH, preferred_element_type=F32)
    phat_ref[...] = phat
    hi = phat.astype(BF)
    ph2_ref[0:64] = hi
    ph2_ref[64:128] = (phat - hi.astype(F32)).astype(BF)


def q_scale_kernel(near, far, linv_ref, out_ref):
    s = (near[...] + far[...]) * (1.0 / 16.0)
    q = jnp.dot(linv_ref[...], s, precision=HIGH, preferred_element_type=F32).astype(BF)
    for k in range(16):
        out_ref[k] = q


def matrix_kernel(at_ref, ga_ref, gb_ref, ea_ref, eb_ref, m_ref):
    at = at_ref[...]
    for j in range(8):
        g, e = (ga_ref[j], ea_ref[j]) if j < 4 else (gb_ref[j - 4], eb_ref[j - 4])
        m_ref[j] = dot(at, g, 1, 0) * (1.0 / 512.0) + e.astype(F32)


def error_half(ph2_ref, q_ref, m_ref, err_hbm, o_buf, sems, base):
    ph = -(ph2_ref[...].T)
    outs = []
    for k in range(4):
        row = block_row(base + k) * 4
        q = jnp.concatenate([q_ref[row + y] for y in range(4)], axis=1)
        q2 = jnp.concatenate([q, q], axis=0)
        o_buf[k] = (m_ref[base + k] + dot(ph, q2, 1, 0)).astype(BF)
        o = pltpu.make_async_copy(o_buf.at[k], err_hbm.at[:, cols(base + k)], sems.at[k])
        o.start()
        outs.append(o)
    return outs


def error_own_kernel(ph2_ref, q_ref, m_ref, err_hbm, qf_ref, o_buf, sems):
    outs = error_half(ph2_ref, q_ref, m_ref, err_hbm, o_buf, sems, 0)
    row = lax.axis_index("x") * 4
    qf_ref[...] = jnp.concatenate([q_ref[row + y] for y in range(4)], axis=1).astype(F32)
    for o in outs:
        o.wait()


def error_sib_kernel(ph2_ref, q_ref, m_ref, _, err_hbm, o_buf, sems):
    for o in error_half(ph2_ref, q_ref, m_ref, err_hbm, o_buf, sems, 4):
        o.wait()


def in_hbm(v):
    return pltpu.with_memory_space_constraint(v, pltpu.HBM)


def shift(v, axis, k):
    n = lax.axis_size(axis)
    return lax.ppermute(v, axis, [(i, (i + k) % n) for i in range(n)])


def trade(v, axis, flip):
    return lax.ppermute(v, axis, [(i, i ^ 1 if flip else 3 - i) for i in range(4)])


def swap(v):
    return lax.ppermute(v, "core", [(0, 1), (1, 0)])


def ring(v, axis):
    return [v] + [shift(v, axis, k) for k in (1, 2, 3)]


def exchange(v, axes):
    return lax.all_to_all(v, axes, 0, 0, tiled=True)


def on_device(attn_out, grad_top, branch_grad, error_prev, q_prev):
    act = attn_out.reshape(512, 512)
    top = grad_top.reshape(512, 512)
    br = branch_grad.reshape(512, 512)
    err = error_prev.reshape(512, 4096)
    qt = q_prev[0].T

    qv, top, br, sent = pl.pallas_call(
        load_kernel,
        out_shape=(sds((64, 512), F32), sds((512, 512), BF), sds((512, 512), BF), sds((512, 512), BF)),
        in_specs=[HBM] * 3,
        out_specs=(VMEM,) * 4,
        scratch_shapes=[pltpu.SemaphoreType.DMA((3,))],
        cost_estimate=LIGHT,
        compiler_params=params(4),
        name="load_kernel",
    )(*(in_hbm(v) for v in (qt, top, br)))

    recv = lax.ppermute(sent, "pipe", [(1, 0)])
    qx = ring(qt, "x")
    err, *_ = lax.optimization_barrier((in_hbm(err), *qx[1:]))
    eh, err, act = pl.pallas_call(
        load_error_kernel,
        out_shape=(sds((4, 512, 512), BF), sds((4, 512, 512), BF), sds((512, 512), BF)),
        in_specs=[HBM] * 2,
        out_specs=(VMEM,) * 3,
        scratch_shapes=[pltpu.SemaphoreType.DMA((9,))],
        cost_estimate=LIGHT,
        compiler_params=params(12),
        name="load_error_kernel",
    )(err, in_hbm(act))
    recv, err = lax.optimization_barrier((recv, err))

    grad, u = pl.pallas_call(
        u_kernel,
        out_shape=(sds((512, 512), BF), sds((64, 512), F32)),
        in_specs=[VMEM] * 3,
        out_specs=(VMEM,) * 2,
        cost_estimate=LIGHT,
        compiler_params=params(6),
        name="u_kernel",
    )(top, recv, qv)
    grad_in = pl.pallas_call(
        grad_in_kernel,
        out_shape=sds((512, 512), BF),
        in_specs=[VMEM] * 2,
        out_specs=VMEM,
        cost_estimate=LIGHT,
        compiler_params=params(6),
        name="grad_in_kernel",
    )(grad, br)
    other, grad_in = lax.optimization_barrier((swap(u), grad_in))
    u = u + other
    eh, _ = lax.optimization_barrier((eh, u))
    eh_s = swap(eh)
    us = ring(u, "x")
    eq, eq_sib, act_t = pl.pallas_call(
        eq_kernel,
        out_shape=(sds((64, 512), F32), sds((64, 512), F32), sds((512, 512), BF)),
        in_specs=[VMEM] * 7,
        out_specs=(VMEM,) * 3,
        cost_estimate=LIGHT,
        compiler_params=params(12),
        name="eq_kernel",
    )(qv, *qx[1:], act, err, eh_s)
    eqs = swap(eq_sib)

    part = pl.pallas_call(
        p_kernel,
        out_shape=sds((64, 512), F32),
        in_specs=[VMEM] * 7,
        out_specs=VMEM,
        cost_estimate=LIGHT,
        compiler_params=params(6),
        name="p_kernel",
    )(*us, act, eq, eqs)
    ys = ring(part, "y")
    grad, *_ = lax.optimization_barrier((grad, eqs, *us))
    g1 = shift(grad, "x", 1)
    g3 = shift(grad, "x", 3)
    lo, hi = pl.pallas_call(
        sum_kernel,
        out_shape=(sds((64, 256), F32), sds((64, 256), F32)),
        in_specs=[VMEM] * 4,
        out_specs=(VMEM, VMEM),
        cost_estimate=LIGHT,
        compiler_params=params(4),
        name="sum_kernel",
    )(*ys)

    lo_in = trade(lo, "zhi", True)
    hi_in = trade(hi, "zhi", False)
    h1, h3, _ = lax.optimization_barrier((g1, g3, lo_in))
    g2a = shift(h1[:256], "x", 1)
    g2b = shift(h3[256:], "x", 3)
    lo, hi = pl.pallas_call(
        add_kernel,
        out_shape=(sds((64, 256), F32), sds((64, 256), F32)),
        in_specs=[VMEM] * 4,
        out_specs=(VMEM, VMEM),
        cost_estimate=LIGHT,
        compiler_params=params(4),
        name="add_kernel",
    )(lo, lo_in, hi, hi_in)
    lo_in = trade(lo, "zhi", False)
    hi_in = trade(hi, "zhi", True)
    p, v = pl.pallas_call(
        pv_kernel,
        out_shape=(sds((64, 512), F32), sds((64, 512), F32)),
        in_specs=[VMEM] * 5,
        out_specs=(VMEM, VMEM),
        cost_estimate=LIGHT,
        compiler_params=params(4),
        name="pv_kernel",
    )(lo, lo_in, hi, hi_in, act)
    ps = swap(p)
    vs = swap(v)
    q_own_part = pl.pallas_call(
        q_own_kernel,
        out_shape=sds((4, 64, 512), F32),
        in_specs=[VMEM] * 2,
        out_specs=VMEM,
        cost_estimate=LIGHT,
        compiler_params=params(8),
        name="q_own_kernel",
    )(p, err)
    chunks, gs = pl.pallas_call(
        q_kernel,
        out_shape=(sds((4, 4, 72, 128), F32), sds((4, 512, 512), BF)),
        in_specs=[VMEM] * 11,
        out_specs=(VMEM, VMEM),
        scratch_shapes=[pltpu.VMEM((32, 128), F32)],
        cost_estimate=LIGHT,
        compiler_params=params(12),
        name="q_kernel",
    )(p, v, ps, vs, q_own_part, eh_s, grad, g1, g2a, g2b, g3)
    gb = swap(gs)
    chunks = exchange(chunks.reshape(16, 72, 128), ("x", "y"))

    q_part, gram = pl.pallas_call(
        chunk_sum_kernel,
        out_shape=(sds((64, 128), F32), sds((32, 128), F32)),
        in_specs=[VMEM],
        out_specs=(VMEM, VMEM),
        cost_estimate=LIGHT,
        compiler_params=params(4),
        name="chunk_sum_kernel",
    )(chunks)
    q_in = trade(q_part, "zhi", True)
    phat, ph2, linv = pl.pallas_call(
        factor_kernel,
        out_shape=(sds((64, 512), F32), sds((128, 512), BF), sds((64, 64), F32)),
        in_specs=[VMEM, VMEM],
        out_specs=(VMEM, VMEM, VMEM),
        cost_estimate=LIGHT,
        compiler_params=params(4),
        name="factor_kernel",
    )(gram, p)
    q_in, linv = lax.optimization_barrier((q_in, linv))
    q_part = q_part + q_in
    q_in = trade(q_part, "zhi", False)
    act_t, _ = lax.optimization_barrier((act_t, q_part))
    matrix = pl.pallas_call(
        matrix_kernel,
        out_shape=sds((8, 512, 512), F32),
        in_specs=[VMEM] * 5,
        out_specs=VMEM,
        cost_estimate=LIGHT,
        compiler_params=params(20),
        name="matrix_kernel",
    )(act_t, gs, gb, err, eh)
    q_in, matrix = lax.optimization_barrier((q_in, matrix))
    q16 = pl.pallas_call(
        q_scale_kernel,
        out_shape=sds((16, 64, 128), BF),
        in_specs=[VMEM] * 3,
        out_specs=VMEM,
        cost_estimate=LIGHT,
        compiler_params=params(4),
        name="q_scale_kernel",
    )(q_part, q_in, linv)
    qfa = exchange(q16, ("x", "y"))
    qfb = swap(qfa)

    scratch = [pltpu.VMEM((4, 512, 512), BF), pltpu.SemaphoreType.DMA((4,))]
    error_next, q_own = pl.pallas_call(
        error_own_kernel,
        out_shape=(sds((512, 4096), BF), sds((64, 512), F32)),
        in_specs=[VMEM] * 3,
        out_specs=(HBM, VMEM),
        scratch_shapes=scratch,
        cost_estimate=LIGHT,
        compiler_params=params(14),
        name="error_own_kernel",
    )(ph2, qfa, matrix)
    error_next = pl.pallas_call(
        error_sib_kernel,
        out_shape=sds((512, 4096), BF),
        in_specs=[VMEM] * 3 + [HBM],
        out_specs=HBM,
        scratch_shapes=scratch,
        input_output_aliases={3: 0},
        cost_estimate=LIGHT,
        compiler_params=params(14),
        name="error_sib_kernel",
    )(ph2, qfb, matrix, error_next)
    return (
        grad_in.reshape(branch_grad.shape),
        error_next.reshape(error_prev.shape),
        phat.T[None],
        q_own.T[None],
    )


def solution(mesh):
    fine = Mesh(mesh.devices.reshape(2, 4, 2, 4, 4), ("pipe", "x", "core", "zhi", "y"))
    tensor = ("x", "core")
    dp = ("zhi", "y")
    return jax.shard_map(
        on_device,
        mesh=fine,
        in_specs=(
            P("pipe", None, dp, tensor),
            P(None, dp, tensor),
            P("pipe", None, dp, tensor),
            P("pipe", dp, tensor, None),
            P("pipe", tensor, None),
        ),
        out_specs=(
            P("pipe", None, dp, tensor),
            P("pipe", dp, tensor, None),
            P("pipe", tensor, None),
            P("pipe", tensor, None),
        ),
        check_vma=False,
    )
```

```python
import jax
import jax.numpy as jnp
from jax import lax
from jax.experimental import pallas as pl
from jax.experimental.pallas import tpu as pltpu
from jax.sharding import Mesh, PartitionSpec as P

BF = jnp.bfloat16
F32 = jnp.float32
HIGH = lax.Precision.HIGHEST
MIB = 1024 * 1024
ANY = pl.BlockSpec(memory_space=pl.ANY)
HBM = pl.BlockSpec(memory_space=pltpu.HBM)
VMEM = pl.BlockSpec(memory_space=pltpu.VMEM)
SMEM = pl.BlockSpec(memory_space=pltpu.SMEM)


LIGHT = pl.CostEstimate(flops=0, transcendentals=0, bytes_accessed=0)


def sds(shape, dtype):
    return jax.ShapeDtypeStruct(shape, dtype)


def params(mib):
    return pltpu.CompilerParams(vmem_limit_bytes=mib * MIB)


def split3(v):
    h = v.astype(BF)
    r = v - h.astype(F32)
    m = r.astype(BF)
    l = (r - m.astype(F32)).astype(BF)
    return jnp.concatenate([h, m, l], axis=0)


def fold3(v):
    n = v.shape[0] // 3
    return v[:n] + (v[n : 2 * n] + v[2 * n :])


def dot(a, b, ca, cb):
    return lax.dot_general(a, b, (((ca,), (cb,)), ((), ())), preferred_element_type=F32)


def u_kernel(top_ref, recv_ref, q_ref, g_ref, u_ref):
    last = lax.axis_index("pipe")

    @pl.when(last == 1)
    def _():
        g_ref[...] = top_ref[...]

    @pl.when(last == 0)
    def _():
        g_ref[...] = recv_ref[...]

    u_ref[...] = fold3(dot(split3(q_ref[...]), g_ref[...], 1, 1))


def grad_in_kernel(g_ref, br_ref, gin_ref):
    gin_ref[...] = (g_ref[...].astype(F32) + br_ref[...].astype(F32)).astype(BF)


def block_row(j):
    return lax.rem(lax.axis_index("x") + 4 - j % 4, 4)


def cols(j, w=512):
    c = lax.axis_index("core")
    owner = block_row(j) * 2 + (c if j < 4 else 1 - c)
    return pl.ds(pl.multiple_of(owner * w, w), w)


def eq_kernel(q0, q1, q2, q3, act_ref, e_ref, es_ref, own_ref, sib_ref, at_ref):
    at_ref[...] = act_ref[...].T
    own = sib = None
    for k, q in enumerate((q0, q1, q2, q3)):
        q3 = split3(q[...])
        a = dot(q3, e_ref[k], 1, 1)
        b = dot(q3, es_ref[k], 1, 1)
        own = a if own is None else own + a
        sib = b if sib is None else sib + b
    own_ref[...] = fold3(own)
    sib_ref[...] = fold3(sib)


def p_kernel(u0, u1, u2, u3, act_ref, eq_ref, eqs_ref, out_ref):
    u = sum_of((u0, u1, u2, u3))
    p = fold3(dot(split3(u), act_ref[...], 1, 0)) * (1.0 / 512.0) + (eq_ref[...] + eqs_ref[...])
    out_ref[...] = p


def sum_of(refs):
    a, b, c, d = refs
    return (a[...] + c[...]) + (b[...] + d[...])


def sum_kernel(a, b, c, d, lo_ref, hi_ref):
    s = sum_of((a, b, c, d))
    lo_ref[...] = s[:, 0:256]
    hi_ref[...] = s[:, 256:512]


def add_kernel(a, b, c, d, ab_ref, cd_ref):
    ab_ref[...] = a[...] + b[...]
    cd_ref[...] = c[...] + d[...]


def put_chunks(out_ref, slot, r, gram):
    for y in range(4):
        out_ref[slot, y, 0:64, :] = r[:, y * 128 : (y + 1) * 128]
        out_ref[slot, y, 64:72, :] = gram


def run_copies(pairs, sems):
    cps = [pltpu.make_async_copy(s, d, sems.at[i]) for i, (s, d) in enumerate(pairs)]
    for cp in cps:
        cp.start()
    for cp in cps:
        cp.wait()


def load_kernel(q, top, br, q_v, top_v, br_v, s_v, sems):
    run_copies(((q, q_v), (top, top_v), (br, br_v)), sems)
    s_v[...] = (top_v[...].astype(F32) + br_v[...].astype(F32)).astype(BF)


def load_error_kernel(e, act, eh_v, e_v, act_v, sems):
    pairs = [(e.at[:, cols(4 + k)], eh_v.at[k]) for k in range(4)]
    pairs += [(e.at[:, cols(k)], e_v.at[k]) for k in range(4)]
    run_copies(pairs + [(act, act_v)], sems)


def pv_kernel(lo, lo_far, hi, hi_far, act_ref, p_ref, v_ref):
    p = jnp.concatenate([lo[...] + lo_far[...], hi[...] + hi_far[...]], axis=1) * (1.0 / 16.0)
    p_ref[...] = p
    v_ref[...] = fold3(dot(split3(p), act_ref[...], 1, 1))


def q_own_kernel(p_ref, e_ref, out_ref):
    p3 = split3(p_ref[...])
    for k in range(4):
        out_ref[k] = fold3(dot(p3, e_ref[k], 1, 0))


def q_kernel(p_ref, v_ref, ps_ref, vs_ref, r_ref, es_ref, g0, g1, g2a, g2b, g3, out_ref, gs_ref, gram_scr):
    v3 = split3(v_ref[...] + vs_ref[...])
    q3 = split3(ps_ref[...])

    def gram_of(p3):
        return dot(p3, p3[0:64], 1, 1) + (dot(p3, p3[64:128], 1, 1) + dot(p3, p3[128:192], 1, 1))

    g = fold3(gram_of(split3(p_ref[...])) + gram_of(q3))
    gram_scr[...] = jnp.concatenate([g[0:32], g[32:64]], axis=1)
    gram = gram_scr[pl.ds(pl.multiple_of(lax.axis_index("y") * 8, 8), 8), :]
    for k, gr in enumerate((g0, g1, None, g3)):
        if k == 2:
            vg = dot(v3[:, 0:256], g2a[...], 1, 0) + dot(v3[:, 256:512], g2b[...], 1, 0)
            gs_ref[k, 0:256] = g2a[...]
            gs_ref[k, 256:512] = g2b[...]
        else:
            vg = dot(v3, gr[...], 1, 0)
            gs_ref[k] = gr[...]
        r = fold3(dot(q3, es_ref[k], 1, 0) + vg * (1.0 / 512.0)) + r_ref[k]
        put_chunks(out_ref, block_row(k), r, gram)


def chunk_sum_kernel(in_ref, q_ref, gram_ref):
    s = in_ref[0, 0:64]
    for k in range(1, 16):
        s = s + in_ref[k, 0:64]
    q_ref[...] = s
    for y in range(4):
        g = (in_ref[y, 64:72] + in_ref[4 + y, 64:72]) + (in_ref[8 + y, 64:72] + in_ref[12 + y, 64:72])
        gram_ref[8 * y : 8 * y + 8] = g


def factor_kernel(gram_ref, p_ref, phat_ref, ph2_ref, linv_ref):
    gp = gram_ref[...]
    n = 64
    left = jnp.concatenate([gp, pltpu.roll(gp, 64, 1)], axis=0)
    row = lax.broadcasted_iota(jnp.int32, (n, 2 * n), 0)
    lane = lax.broadcasted_iota(jnp.int32, (n, 2 * n), 1)
    a = jnp.where(lane < n, left, jnp.where(lane == row + n, 1.0, 0.0))
    for k in range(0, n, 8):
        rows = [a[k + i : k + i + 1, :] for i in range(8)]
        fs = [jnp.broadcast_to(a[:, k + i : k + i + 1], (n, 2 * n)) for i in range(8)]
        for i in range(8):
            d = fs[i][k + i : k + i + 1, :]
            r = lax.rsqrt(d)
            r = r * (1.5 - 0.5 * d * r * r)
            rows[i] = rows[i] * r
            fs[i] = fs[i] * r
            for j in range(i + 1, 8):
                m = fs[i][k + j : k + j + 1, :]
                rows[j] = rows[j] - m * rows[i]
                fs[j] = fs[j] - m * fs[i]
        upd = fs[0] * rows[0]
        for i in range(1, 8):
            upd = upd + fs[i] * rows[i]
        block = jnp.concatenate(rows, axis=0)
        parts = [a[:k]] if k else []
        parts.append(block)
        if k + 8 < n:
            parts.append(a[k + 8 :] - upd[k + 8 :])
        a = jnp.concatenate(parts, axis=0) if len(parts) > 1 else block
    linv = pltpu.roll(a, 64, 1)[:, 0:n]
    linv_ref[...] = linv
    phat = jnp.dot(linv, p_ref[...], precision=HIGH, preferred_element_type=F32)
    phat_ref[...] = phat
    hi = phat.astype(BF)
    lo = (phat - hi.astype(F32)).astype(BF)
    ph2_ref[...] = -(jnp.concatenate([hi, lo], axis=0).T)


def q_scale_kernel(near, far, linv_ref, out_ref):
    s = (near[...] + far[...]) * (1.0 / 16.0)
    q = jnp.dot(linv_ref[...], s, precision=HIGH, preferred_element_type=F32).astype(BF)
    for k in range(16):
        out_ref[k] = q


def matrix_kernel(at_ref, ga_ref, gb_ref, ea_ref, eb_ref, m_ref):
    at = at_ref[...]
    for j in range(8):
        g, e = (ga_ref[j], ea_ref[j]) if j < 4 else (gb_ref[j - 4], eb_ref[j - 4])
        m_ref[j] = dot(at, g, 1, 0) * (1.0 / 512.0) + e.astype(F32)


def error_half(ph2_ref, q_ref, m_ref, err_hbm, o_buf, sems, base):
    ph = ph2_ref[...]
    outs = []
    for k in range(4):
        row = block_row(base + k) * 4
        q = jnp.concatenate([q_ref[row + y] for y in range(4)], axis=1)
        q2 = jnp.concatenate([q, q], axis=0)
        o_buf[k] = (m_ref[base + k] + dot(ph, q2, 1, 0)).astype(BF)
        o = pltpu.make_async_copy(o_buf.at[k], err_hbm.at[:, cols(base + k)], sems.at[k])
        o.start()
        outs.append(o)
    return outs


def error_own_kernel(ph2_ref, q_ref, m_ref, err_hbm, qf_ref, o_buf, sems):
    outs = error_half(ph2_ref, q_ref, m_ref, err_hbm, o_buf, sems, 0)
    row = lax.axis_index("x") * 4
    qf_ref[...] = jnp.concatenate([q_ref[row + y] for y in range(4)], axis=1).astype(F32)
    for o in outs:
        o.wait()


def error_sib_kernel(ph2_ref, q_ref, m_ref, _, err_hbm, o_buf, sems):
    for o in error_half(ph2_ref, q_ref, m_ref, err_hbm, o_buf, sems, 4):
        o.wait()


def in_hbm(v):
    return pltpu.with_memory_space_constraint(v, pltpu.HBM)


def shift(v, axis, k):
    n = lax.axis_size(axis)
    return lax.ppermute(v, axis, [(i, (i + k) % n) for i in range(n)])


def trade(v, axis, flip):
    return lax.ppermute(v, axis, [(i, i ^ 1 if flip else 3 - i) for i in range(4)])


def swap(v):
    return lax.ppermute(v, "core", [(0, 1), (1, 0)])


def ring(v, axis):
    return [v] + [shift(v, axis, k) for k in (1, 2, 3)]


def exchange(v, axes):
    return lax.all_to_all(v, axes, 0, 0, tiled=True)


def on_device(attn_out, grad_top, branch_grad, error_prev, q_prev):
    act = attn_out.reshape(512, 512)
    top = grad_top.reshape(512, 512)
    br = branch_grad.reshape(512, 512)
    err = error_prev.reshape(512, 4096)
    qt = q_prev[0].T

    qv, top, br, sent = pl.pallas_call(
        load_kernel,
        out_shape=(sds((64, 512), F32), sds((512, 512), BF), sds((512, 512), BF), sds((512, 512), BF)),
        in_specs=[HBM] * 3,
        out_specs=(VMEM,) * 4,
        scratch_shapes=[pltpu.SemaphoreType.DMA((3,))],
        cost_estimate=LIGHT,
        compiler_params=params(4),
        name="load_kernel",
    )(*(in_hbm(v) for v in (qt, top, br)))

    recv = lax.ppermute(sent, "pipe", [(1, 0)])
    qx = ring(qt, "x")
    err, *_ = lax.optimization_barrier((in_hbm(err), *qx[1:]))
    eh, err, act = pl.pallas_call(
        load_error_kernel,
        out_shape=(sds((4, 512, 512), BF), sds((4, 512, 512), BF), sds((512, 512), BF)),
        in_specs=[HBM] * 2,
        out_specs=(VMEM,) * 3,
        scratch_shapes=[pltpu.SemaphoreType.DMA((9,))],
        cost_estimate=LIGHT,
        compiler_params=params(12),
        name="load_error_kernel",
    )(err, in_hbm(act))
    recv, err = lax.optimization_barrier((recv, err))

    grad, u = pl.pallas_call(
        u_kernel,
        out_shape=(sds((512, 512), BF), sds((64, 512), F32)),
        in_specs=[VMEM] * 3,
        out_specs=(VMEM,) * 2,
        cost_estimate=LIGHT,
        compiler_params=params(6),
        name="u_kernel",
    )(top, recv, qv)
    u = u + swap(u)
    eh, _ = lax.optimization_barrier((eh, u))
    eh_s = swap(eh)
    us = ring(u, "x")
    eq, eq_sib, act_t = pl.pallas_call(
        eq_kernel,
        out_shape=(sds((64, 512), F32), sds((64, 512), F32), sds((512, 512), BF)),
        in_specs=[VMEM] * 7,
        out_specs=(VMEM,) * 3,
        cost_estimate=LIGHT,
        compiler_params=params(12),
        name="eq_kernel",
    )(qv, *qx[1:], act, err, eh_s)
    eqs = swap(eq_sib)
    br, _ = lax.optimization_barrier((br, eq))
    grad_in = pl.pallas_call(
        grad_in_kernel,
        out_shape=sds((512, 512), BF),
        in_specs=[VMEM] * 2,
        out_specs=VMEM,
        cost_estimate=LIGHT,
        compiler_params=params(6),
        name="grad_in_kernel",
    )(grad, br)
    eqs, grad_in = lax.optimization_barrier((eqs, grad_in))

    part = pl.pallas_call(
        p_kernel,
        out_shape=sds((64, 512), F32),
        in_specs=[VMEM] * 7,
        out_specs=VMEM,
        cost_estimate=LIGHT,
        compiler_params=params(6),
        name="p_kernel",
    )(*us, act, eq, eqs)
    ys = ring(part, "y")
    grad, *_ = lax.optimization_barrier((grad, eqs, *us))
    g1 = shift(grad, "x", 1)
    g3 = shift(grad, "x", 3)
    lo, hi = pl.pallas_call(
        sum_kernel,
        out_shape=(sds((64, 256), F32), sds((64, 256), F32)),
        in_specs=[VMEM] * 4,
        out_specs=(VMEM, VMEM),
        cost_estimate=LIGHT,
        compiler_params=params(4),
        name="sum_kernel",
    )(*ys)

    lo_in = trade(lo, "zhi", True)
    hi_in = trade(hi, "zhi", False)
    h1, h3, _ = lax.optimization_barrier((g1, g3, lo_in))
    g2a = shift(h1[:256], "x", 1)
    g2b = shift(h3[256:], "x", 3)
    lo, hi = pl.pallas_call(
        add_kernel,
        out_shape=(sds((64, 256), F32), sds((64, 256), F32)),
        in_specs=[VMEM] * 4,
        out_specs=(VMEM, VMEM),
        cost_estimate=LIGHT,
        compiler_params=params(4),
        name="add_kernel",
    )(lo, lo_in, hi, hi_in)
    lo_in = trade(lo, "zhi", False)
    hi_in = trade(hi, "zhi", True)
    p, v = pl.pallas_call(
        pv_kernel,
        out_shape=(sds((64, 512), F32), sds((64, 512), F32)),
        in_specs=[VMEM] * 5,
        out_specs=(VMEM, VMEM),
        cost_estimate=LIGHT,
        compiler_params=params(4),
        name="pv_kernel",
    )(lo, lo_in, hi, hi_in, act)
    ps = swap(p)
    vs = swap(v)
    q_own_part = pl.pallas_call(
        q_own_kernel,
        out_shape=sds((4, 64, 512), F32),
        in_specs=[VMEM] * 2,
        out_specs=VMEM,
        cost_estimate=LIGHT,
        compiler_params=params(8),
        name="q_own_kernel",
    )(p, err)
    chunks, gs = pl.pallas_call(
        q_kernel,
        out_shape=(sds((4, 4, 72, 128), F32), sds((4, 512, 512), BF)),
        in_specs=[VMEM] * 11,
        out_specs=(VMEM, VMEM),
        scratch_shapes=[pltpu.VMEM((32, 128), F32)],
        cost_estimate=LIGHT,
        compiler_params=params(12),
        name="q_kernel",
    )(p, v, ps, vs, q_own_part, eh_s, grad, g1, g2a, g2b, g3)
    gb = swap(gs)
    chunks = exchange(chunks.reshape(16, 72, 128), ("x", "y"))

    q_part, gram = pl.pallas_call(
        chunk_sum_kernel,
        out_shape=(sds((64, 128), F32), sds((32, 128), F32)),
        in_specs=[VMEM],
        out_specs=(VMEM, VMEM),
        cost_estimate=LIGHT,
        compiler_params=params(4),
        name="chunk_sum_kernel",
    )(chunks)
    q_in = trade(q_part, "zhi", True)
    phat, ph2, linv = pl.pallas_call(
        factor_kernel,
        out_shape=(sds((64, 512), F32), sds((512, 128), BF), sds((64, 64), F32)),
        in_specs=[VMEM, VMEM],
        out_specs=(VMEM, VMEM, VMEM),
        cost_estimate=LIGHT,
        compiler_params=params(4),
        name="factor_kernel",
    )(gram, p)
    q_in, linv = lax.optimization_barrier((q_in, linv))
    q_part = q_part + q_in
    q_in = trade(q_part, "zhi", False)
    act_t, _ = lax.optimization_barrier((act_t, q_part))
    matrix = pl.pallas_call(
        matrix_kernel,
        out_shape=sds((8, 512, 512), F32),
        in_specs=[VMEM] * 5,
        out_specs=VMEM,
        cost_estimate=LIGHT,
        compiler_params=params(20),
        name="matrix_kernel",
    )(act_t, gs, gb, err, eh)
    q_in, matrix = lax.optimization_barrier((q_in, matrix))
    q16 = pl.pallas_call(
        q_scale_kernel,
        out_shape=sds((16, 64, 128), BF),
        in_specs=[VMEM] * 3,
        out_specs=VMEM,
        cost_estimate=LIGHT,
        compiler_params=params(4),
        name="q_scale_kernel",
    )(q_part, q_in, linv)
    qfa = exchange(q16, ("x", "y"))
    qfb = swap(qfa)

    scratch = [pltpu.VMEM((4, 512, 512), BF), pltpu.SemaphoreType.DMA((4,))]
    error_next, q_own = pl.pallas_call(
        error_own_kernel,
        out_shape=(sds((512, 4096), BF), sds((64, 512), F32)),
        in_specs=[VMEM] * 3,
        out_specs=(HBM, VMEM),
        scratch_shapes=scratch,
        cost_estimate=LIGHT,
        compiler_params=params(14),
        name="error_own_kernel",
    )(ph2, qfa, matrix)
    error_next = pl.pallas_call(
        error_sib_kernel,
        out_shape=sds((512, 4096), BF),
        in_specs=[VMEM] * 3 + [HBM],
        out_specs=HBM,
        scratch_shapes=scratch,
        input_output_aliases={3: 0},
        cost_estimate=LIGHT,
        compiler_params=params(14),
        name="error_sib_kernel",
    )(ph2, qfb, matrix, error_next)
    return (
        grad_in.reshape(branch_grad.shape),
        error_next.reshape(error_prev.shape),
        phat.T[None],
        q_own.T[None],
    )


def solution(mesh):
    fine = Mesh(mesh.devices.reshape(2, 4, 2, 4, 4), ("pipe", "x", "core", "zhi", "y"))
    tensor = ("x", "core")
    dp = ("zhi", "y")
    return jax.shard_map(
        on_device,
        mesh=fine,
        in_specs=(
            P("pipe", None, dp, tensor),
            P(None, dp, tensor),
            P("pipe", None, dp, tensor),
            P("pipe", dp, tensor, None),
            P("pipe", tensor, None),
        ),
        out_specs=(
            P("pipe", None, dp, tensor),
            P("pipe", dp, tensor, None),
            P("pipe", tensor, None),
            P("pipe", tensor, None),
        ),
        check_vma=False,
    )
```
